128 devices in a mesh: circ: 8 (over z_lo, x), axial: 16 (over y, z_hi, core).
Axes of the slice: x: 4, y: 4, z: 4 (z_hi: 2, z_lo: 2; z = z_hi * 2 + z_lo), core: 2. Of those that a mesh axis runs over, the one named last changes fastest.
Arguments:
- calcium: float32 [2, 1024, 4096], P(None, 'circ', 'axial'), may hold values from 0.1 to 3
- voltage: float32 [2, 1024, 4096], P(None, 'circ', 'axial'), may hold values from -1.5 to 0.5
- conductance: float32 [1024, 4096], P('circ', 'axial'), may hold values from 0.5 to 2
- fluid_blocks: float32 [24576, 2, 256], P(('circ', 'axial')), may hold values from -9 to 9
- target_device: int32 [24576, 1], P(('circ', 'axial')), may hold values from 0 to 127; in each aligned block of 192 rows (0 to 191, 192 to 383, ...) at most 2 rows name the same one
- target_row: int32 [24576], P(('circ', 'axial')), may hold values from 0 to 127
- block_counts: int32 [128], P(('circ', 'axial')), may hold values from 96 to 192
- port_cells: int32 [1024], P(('circ', 'axial')), may hold values from 0 to 32767
- partner: int32 [1024], P(('circ', 'axial')), may hold values from 0 to 1023, each once
Outputs:
- calcium_out: float32 [2, 1024, 4096], P(None, 'circ', 'axial')
- voltage_out: float32 [2, 1024, 4096], P(None, 'circ', 'axial')
The draws below stay inside these ranges and needn't reach their ends.
Inputs may be any that keep to these rules, and one draw needn't show every extreme that they name: `target_device`: among the 192 slots of one device, used or not, no device number appears more than 2 times, and some number appears exactly 2 times. Only a device's first block_counts slots are used. `port_cells`: ports may share a cell.
All inputs are finite; a program needn't handle non-finite values.
Results may differ from the reference program's by a relative error of at most 0.00002.
Values sent between devices are 32-bit elements; how exact they have to be, the bound alone decides.
No kernel may reach another device: no remote copies, remote signals or barrier semaphores. Data moves between devices by JAX's collectives and lax.ppermute only.
A program may use at most 64 MiB of HBM per device.

```python
import math
import jax
import jax.numpy as jnp
import numpy as np

CC = 128
CA = 256
ITERS = 8
SLOT = 2
JN_DEV = 8
FB_DEV = 192
FB_TOTAL = 24576
PORTS = 1024
NC = 1024
NA = 4096
N_AXIAL = 16
DEVICES = 128


def set_ends(entries, rng, smallest, top_value):
    spot = [jax.random.randint(jax.random.fold_in(rng, axis), (), 0, length) for axis, length in enumerate(entries.shape)]
    main_axis = entries.shape.index(max(entries.shape))
    neighbour = spot[:main_axis] + [(spot[main_axis] + 1) % entries.shape[main_axis]] + spot[main_axis + 1:]
    return entries.at[tuple(spot)].set(smallest).at[tuple(neighbour)].set(top_value)


def shard_levels(key, dims, pieces, smallest, high):
    def one(position, blocks):
        steps = jax.random.uniform(jax.random.fold_in(jax.random.fold_in(key, 6), position), (blocks,), jnp.float32, smallest / len(pieces), high / len(pieces))
        return jnp.repeat(jnp.exp(steps), dims[position] // blocks).reshape((-1,) + (1,) * (len(dims) - position - 1))

    level = one(*pieces[0])
    for cut in pieces[1:]:
        level = level * one(*cut)
    return level


def assign_block(own_key, own, number, rows, count, top, bound, slope):
    sequence = jax.random.permutation(own_key, count)
    heavy_load, usual = portions_of(count, rows * top, bound, slope, True), portions_of(count, rows * top, bound, slope, False)
    places = jnp.arange(count)

    def named(sizes, turn):
        used = int((sizes > 0).sum())
        fixed = max(1, used // 4)
        passed = fixed + (places - fixed + turn * (used - fixed)) % max(1, count - fixed)
        return jnp.zeros((count,), jnp.int32).at[sequence[jnp.where(places < fixed, places, passed)]].set(jnp.asarray(sizes, jnp.int32))

    sizes = jnp.where(number % 4 == 0, named(heavy_load, number // 4), named(usual, number - number // 4 - 1))
    mixed = jax.random.permutation(jax.random.fold_in(own, 3), count)
    donor, sink = mixed[0:count // 2 * 2:2], mixed[1:count // 2 * 2:2]
    room = jnp.minimum(sizes[donor] - 1, bound - sizes[sink]) // 2
    room = jnp.where((donor == sequence[0]) | (sink == sequence[0]) | (sizes[sink] == 0), 0, jnp.maximum(room, 0))
    passed = jax.random.randint(jax.random.fold_in(own, 4), (count // 2,), 0, 1 << 20) % (room + 1)
    sizes = sizes.at[donor].add(-passed).at[sink].add(passed)
    items = jnp.searchsorted(jnp.cumsum(sizes), jnp.arange(rows * top), side="right").astype(jnp.int32)
    listing = items.reshape(top, rows).T
    listing = listing[jax.random.permutation(jax.random.fold_in(own, 1), rows)]
    turn = jax.random.randint(jax.random.fold_in(own, 2), (rows, 1), 0, top)
    return jnp.take_along_axis(listing, (jnp.arange(top)[None, :] + turn) % top, axis=1)


def portions_of(number_of, total, limit, slope, full):
    weights = [(1 << 20) // math.isqrt(rank ** slope) + 1 for rank in range(1, number_of + 1)]
    largest = limit if full else min(limit, max(-(-total // number_of), total * weights[0] // sum(weights)))
    least = 1 if total - largest >= number_of - 1 else 0
    holding, spare = [largest] + [least] * (number_of - 1), total - largest - least * (number_of - 1)
    while spare > 0:
        candidates = [i for i in range(1, number_of) if holding[i] < largest] or [i for i in range(1, number_of) if holding[i] < limit]
        mass, budget = sum([weights[i] for i in candidates]), spare
        for i in candidates:
            addition = min(limit - holding[i], max(1, budget * weights[i] // mass), spare)
            holding[i] = holding[i] + addition
            spare = spare - addition
    return np.array(holding)


def noise(key, dims, width, reach, split=(), kind=jnp.bfloat16):
    values = width * jax.random.normal(key, dims, jnp.float32)
    if split:
        values = values * shard_levels(key, dims, split, -0.22, 0.18)
    return jnp.clip(values, -reach, reach).astype(kind)


def setup_inputs(seed: int = 0) -> dict:
    splits = jax.random.split(jax.random.key(seed), 10)
    calcium = jnp.clip(jnp.exp(math.log(3.0) - 3.4011974 * jax.random.uniform(splits[0], (2, NC, NA), jnp.float32) ** shard_levels(splits[0], (2, NC, NA), ((1, 8), (2, 16)), -0.2, 0.2)), 0.1, 3.0)
    voltage = jnp.clip(-1.5 + 2.0 * jax.random.uniform(splits[1], (2, NC, NA), jnp.float32) ** shard_levels(splits[1], (2, NC, NA), ((1, 8), (2, 16)), -0.2, 0.2), -1.5, 0.5)
    conductance = jnp.clip(jnp.exp(math.log(2.0) - 1.3862944 * jax.random.uniform(splits[2], (NC, NA), jnp.float32) ** shard_levels(splits[2], (NC, NA), ((0, 8), (1, 16)), -0.2, 0.2)), 0.5, 2.0)
    fluid_blocks = noise(splits[3], (FB_TOTAL, 2, CA), 1.5, 9.0, ((0, 128),), jnp.float32)
    target_device_keys = jax.random.split(jax.random.fold_in(splits[4], 1), FB_TOTAL // FB_DEV)
    target_device_turns = jax.random.permutation(jax.random.fold_in(splits[4], 3), FB_TOTAL // FB_DEV)
    target_device = jax.vmap(lambda own, number: assign_block(jax.random.fold_in(splits[4], 2), own, number, FB_DEV, DEVICES, 1, SLOT, 1))(target_device_keys, target_device_turns).reshape((FB_TOTAL, 1))
    target_row = set_ends(jax.random.randint(splits[5], (FB_TOTAL,), 0, CC), jax.random.fold_in(splits[5], 1), 0, CC - 1).astype(jnp.int32)
    block_counts = set_ends(jax.random.randint(splits[6], (DEVICES,), FB_DEV // 2, FB_DEV + 1), jax.random.fold_in(splits[6], 1), FB_DEV // 2, FB_DEV).astype(jnp.int32)
    port_cells = set_ends(jax.random.randint(splits[7], (PORTS,), 0, CC * CA), jax.random.fold_in(splits[7], 1), 0, (CC * CA) - 1).astype(jnp.int32)
    partner = jax.random.permutation(splits[8], PORTS).astype(jnp.int32)
    return {"calcium": calcium, "voltage": voltage, "conductance": conductance, "fluid_blocks": fluid_blocks, "target_device": target_device, "target_row": target_row, "block_counts": block_counts, "port_cells": port_cells, "partner": partner}


rate_step = 0.1
couple_step = 0.05
junction_step = 0.2


def advance(calcium, voltage, near_calcium, near_voltage, spread, stress, stimulus):
    smc_ca = calcium[0]
    end_ca = calcium[1]
    smc_volt = voltage[0]
    end_volt = voltage[1]
    new_smc_ca = smc_ca + rate_step * (0.8 * jax.nn.sigmoid(2.0 * (smc_volt + 0.3)) + stimulus - 1.2 * smc_ca / (smc_ca + 0.5) + 0.3 * (end_ca - smc_ca)) + spread * (near_calcium[0] - 4.0 * smc_ca)
    new_end_ca = end_ca + rate_step * (0.2 + 1.5 * stress + 0.4 * stimulus - 0.9 * end_ca + 0.3 * (smc_ca - end_ca)) + spread * (near_calcium[1] - 4.0 * end_ca)
    new_smc_volt = smc_volt + rate_step * (-(smc_volt + 0.5) - 1.5 * smc_ca / (smc_ca + 1.0) * (smc_volt + 1.2) + 0.4 * (end_volt - smc_volt)) + spread * (near_voltage[0] - 4.0 * smc_volt)
    new_end_volt = end_volt + rate_step * (-0.8 * (end_volt + 0.4) - end_ca / (end_ca + 1.0) * (end_volt + 1.2) + 0.4 * (smc_volt - end_volt)) + spread * (near_voltage[1] - 4.0 * end_volt)
    return jnp.stack([new_smc_ca, new_end_ca]), jnp.stack([new_smc_volt, new_end_volt])


def neighbours(fields):
    padded = jnp.pad(fields, ((0, 0), (0, 0), (1, 1)), mode="edge")
    return jnp.roll(fields, 1, axis=1) + jnp.roll(fields, -1, axis=1) + padded[:, :, :-2] + padded[:, :, 2:]


def reference(calcium, voltage, conductance, fluid_blocks, target_device, target_row, block_counts, port_cells, partner):
    slots = jnp.arange(FB_TOTAL, dtype=jnp.int32)
    source = slots // FB_DEV
    active = (slots % FB_DEV) < block_counts[source]
    target = target_device[:, 0]
    cycle_idx = target // N_AXIAL
    strip_idx = target % N_AXIAL
    global_row = cycle_idx * CC + target_row
    block_id = (global_row * N_AXIAL + strip_idx).astype(jnp.int32)
    weighted = fluid_blocks * active[:, None, None].astype(jnp.float32)
    summed = jnp.zeros((NC * N_AXIAL, 2, CA), jnp.float32).at[block_id].add(weighted)
    forcing = jnp.transpose(summed.reshape(NC, N_AXIAL, 2, CA), (2, 0, 1, 3)).reshape(2, NC, NA)
    shear = forcing[0]
    agonist = forcing[1]
    stress = shear * shear / (1.0 + shear * shear)
    stimulus = jax.nn.sigmoid(agonist)
    spread = couple_step * conductance
    port_dev = jnp.arange(PORTS, dtype=jnp.int32) // JN_DEV
    port_row = (port_dev // N_AXIAL) * CC + port_cells // CA
    port_col = (port_dev % N_AXIAL) * CA + port_cells % CA
    for substep in range(ITERS):
        port_values = voltage[0][port_row, port_col]
        gain_term = junction_step * (port_values[partner] - port_values)
        calcium_new, voltage_new = advance(calcium, voltage, neighbours(calcium), neighbours(voltage), spread, stress, stimulus)
        smc_volt = voltage_new[0].at[port_row, port_col].add(gain_term)
        voltage = jnp.stack([smc_volt, voltage_new[1]])
        calcium = calcium_new
    return calcium, voltage
```

```python
import jax
import jax.numpy as jnp
from jax import lax
from jax.sharding import PartitionSpec as P

ITERS = 8
SLOT = 2
JN_DEV = 8


rate_step = 0.1
couple_step = 0.05
junction_step = 0.2


def padded(block, sides, width, periodic):
    for axis, dim in sides:
        count = lax.axis_size(axis)
        forward = [(i, i + 1) for i in range(count - 1)]
        if periodic:
            forward.append((count - 1, 0))
        backward = [(target, source) for source, target in forward]
        low = lax.ppermute(
            lax.slice_in_dim(block, block.shape[dim] - width, None, axis=dim), axis, forward
        )
        high = lax.ppermute(lax.slice_in_dim(block, 0, width, axis=dim), axis, backward)
        block = jnp.concatenate([low, block, high], axis=dim)
    return block


def split_up(value, dim, size):
    before, after = (value.shape[:dim], value.shape[dim + 1 :])
    return jnp.moveaxis(value.reshape(*before, size, -1, *after), dim, 0)


def joined_along(pieces, dim):
    pieces = jnp.moveaxis(pieces, 0, dim)
    shape = pieces.shape
    return pieces.reshape(*shape[:dim], shape[dim] * shape[dim + 1], *shape[dim + 2 :])


def one_exchange(value, axis, axes, splits, concats):
    sizes = [lax.axis_size(a) for a in axes]
    pieces = split_up(value, splits[0], sizes[0])
    pieces = jnp.moveaxis(split_up(pieces, splits[1] + 1, sizes[1]), 0, 1)
    inside = pieces.shape[2:]
    pieces = pieces.reshape(-1, *inside)
    pieces = lax.all_to_all(pieces, axis, split_axis=0, concat_axis=0, tiled=True)
    pieces = joined_along(pieces.reshape(*sizes, *inside), concats[0] + 1)
    return joined_along(pieces, concats[1])


def advance(calcium, voltage, near_calcium, near_voltage, spread, stress, stimulus):
    smc_ca = calcium[0]
    end_ca = calcium[1]
    smc_volt = voltage[0]
    end_volt = voltage[1]
    new_smc_ca = (
        smc_ca
        + rate_step
        * (
            0.8 * jax.nn.sigmoid(2.0 * (smc_volt + 0.3))
            + stimulus
            - 1.2 * smc_ca / (smc_ca + 0.5)
            + 0.3 * (end_ca - smc_ca)
        )
        + spread * (near_calcium[0] - 4.0 * smc_ca)
    )
    new_end_ca = (
        end_ca
        + rate_step * (0.2 + 1.5 * stress + 0.4 * stimulus - 0.9 * end_ca + 0.3 * (smc_ca - end_ca))
        + spread * (near_calcium[1] - 4.0 * end_ca)
    )
    new_smc_volt = (
        smc_volt
        + rate_step
        * (
            -(smc_volt + 0.5)
            - 1.5 * smc_ca / (smc_ca + 1.0) * (smc_volt + 1.2)
            + 0.4 * (end_volt - smc_volt)
        )
        + spread * (near_voltage[0] - 4.0 * smc_volt)
    )
    new_end_volt = (
        end_volt
        + rate_step
        * (
            -0.8 * (end_volt + 0.4)
            - end_ca / (end_ca + 1.0) * (end_volt + 1.2)
            + 0.4 * (smc_volt - end_volt)
        )
        + spread * (near_voltage[1] - 4.0 * end_volt)
    )
    return (jnp.stack([new_smc_ca, new_end_ca]), jnp.stack([new_smc_volt, new_end_volt]))


def neighbours(fields):
    cycle_pad = padded(fields, (("circ", 1),), 1, True)
    strip_pad = padded(fields, (("axial", 2),), 1, False)
    first = lax.axis_index("axial") == 0
    final = lax.axis_index("axial") == lax.axis_size("axial") - 1
    left_side = strip_pad[:, :, :-2]
    right_side = strip_pad[:, :, 2:]
    left_side = left_side.at[:, :, 0].set(jnp.where(first, fields[:, :, 0], left_side[:, :, 0]))
    right_side = right_side.at[:, :, -1].set(
        jnp.where(final, fields[:, :, -1], right_side[:, :, -1])
    )
    return cycle_pad[:, :-2] + cycle_pad[:, 2:] + left_side + right_side


def local(
    calcium,
    voltage,
    conductance,
    fluid_blocks,
    target_device,
    target_row,
    block_counts,
    port_cells,
    partner,
):
    cycle_count = lax.axis_size("circ")
    strip_count = lax.axis_size("axial")
    devices = cycle_count * strip_count
    slot_count = fluid_blocks.shape[0]
    width = fluid_blocks.shape[2]
    row_count = conductance.shape[0]
    order_idx = jnp.arange(slot_count, dtype=jnp.int32)
    active = order_idx < block_counts[0]
    target = target_device[:, 0]
    earlier = (
        (target[:, None] == target[None, :])
        & active[None, :]
        & (order_idx[None, :] < order_idx[:, None])
    )
    slot_rank = jnp.sum(earlier.astype(jnp.int32), axis=1)
    position = jnp.where(active, target * SLOT + slot_rank, devices * SLOT)
    outgoing = (
        jnp.zeros((devices * SLOT, 2, width), jnp.float32)
        .at[position]
        .set(fluid_blocks, mode="drop")
    )
    row_tags = (
        jnp.full((devices * SLOT,), row_count, jnp.int32).at[position].set(target_row, mode="drop")
    )
    received, recv_rows = (
        one_exchange(
            outgoing.reshape(cycle_count, strip_count, SLOT, 2, width),
            ("circ", "axial"),
            ("circ", "axial"),
            (0, 1),
            (0, 1),
        ),
        one_exchange(
            row_tags.reshape(cycle_count, strip_count, SLOT),
            ("circ", "axial"),
            ("circ", "axial"),
            (0, 1),
            (0, 1),
        ),
    )
    received = received.reshape(devices * SLOT, 2, width)
    recv_rows = recv_rows.reshape(devices * SLOT)
    forcing = jnp.zeros((row_count, 2, width), jnp.float32).at[recv_rows].add(received, mode="drop")
    shear = forcing[:, 0]
    agonist = forcing[:, 1]
    stress = shear * shear / (1.0 + shear * shear)
    stimulus = jax.nn.sigmoid(agonist)
    spread = couple_step * conductance
    for substep in range(ITERS):
        flat_volt = voltage[0].reshape(-1)
        port_values = flat_volt[port_cells]
        copies = jnp.broadcast_to(port_values[None, None], (devices, 1, JN_DEV))
        all_ports = lax.all_to_all(copies, ("circ", "axial"), 0, 0, tiled=True).reshape(-1)
        gain_term = junction_step * (all_ports[partner] - port_values)
        calcium_new, voltage_new = advance(
            calcium, voltage, neighbours(calcium), neighbours(voltage), spread, stress, stimulus
        )
        smc_volt = (
            voltage_new[0].reshape(-1).at[port_cells].add(gain_term).reshape(voltage_new[0].shape)
        )
        voltage = jnp.stack([smc_volt, voltage_new[1]])
        calcium = calcium_new
    return (calcium, voltage)


def solution(mesh):
    return jax.shard_map(
        local,
        mesh=mesh,
        in_specs=(
            P(None, "circ", "axial"),
            P(None, "circ", "axial"),
            P("circ", "axial"),
            P(("circ", "axial"), None, None),
            P(("circ", "axial"), None),
            P(("circ", "axial")),
            P(("circ", "axial")),
            P(("circ", "axial")),
            P(("circ", "axial")),
        ),
        out_specs=(P(None, "circ", "axial"), P(None, "circ", "axial")),
        check_vma=False,
    )
```

```python
import functools

import jax
import jax.numpy as jnp
import numpy as np
from jax import lax
from jax.experimental import pallas as pl
from jax.experimental.pallas import tpu as pltpu
from jax.sharding import PartitionSpec as P

AXES = ("circ", "axial")
HALO = 8
LANES = 128
WIDE = 384
TOP = 16
EXT = 160
NEAR_LANES = (0, 1, -1, 16, -16, 15, -15, 17, -17)
ROW_KEY = 8192
KEY_MASK = 1024 * ROW_KEY - 1
HIGH = lax.Precision.HIGHEST
VMEM = pl.BlockSpec(memory_space=pltpu.VMEM)
SMEM = pl.BlockSpec(memory_space=pltpu.SMEM)


def diamond(radius):
    if radius < 0:
        return []
    span = range(-radius, radius + 1)
    return [(a, b) for a in span for b in span if abs(a) + abs(b) <= radius]


def patch_plan(radius):
    radii = (radius, radius - 1, radius - 1, radius - 1, radius - 2, radius - 2, radius - 3)
    return [(field, cell) for field, r in enumerate(radii) for cell in diamond(r)]


def patch_tables(radius):
    plan = patch_plan(radius)
    side = 2 * radius + 1
    deep = -(-side // 8) * 8
    width = -(-len(plan) * 8 // LANES) * LANES
    table = np.full((8, width), -1, np.int32)
    for index, (field, (a, b)) in enumerate(plan):
        for slot in range(8):
            at = index * 8 + slot
            table[0, at] = field * side + b + radius
            table[1, at] = slot * deep + a + radius
    return table


def iota(shape, dim):
    return lax.broadcasted_iota(jnp.int32, shape, dim)


def call(kernel, outs, ins, name, scratch=()):
    return pl.pallas_call(
        kernel,
        out_shape=tuple(jax.ShapeDtypeStruct(s, jnp.float32) for s in outs),
        in_specs=ins,
        out_specs=tuple(VMEM for _ in outs),
        scratch_shapes=list(scratch),
        name=name,
    )


def side_strips(tiles):
    rows = tiles[0][0].shape[0]
    lane = iota((rows, LANES), 1)
    left = jnp.zeros((rows, LANES), jnp.float32)
    right = left
    for f, (first, last) in enumerate(tiles):
        mine = (lane >= f * HALO) & (lane < (f + 1) * HALO)
        left = jnp.where(mine, pltpu.roll(first, f * HALO, 1) if f else first, left)
        right = jnp.where(mine, pltpu.roll(last, f * HALO + HALO, 1), right)
    return left, right


def side_tile(from_east, from_west, f):
    lane = iota(from_east.shape, 1)
    east = pltpu.roll(from_east, (LANES - f * HALO) % LANES, 1) if f else from_east
    west = pltpu.roll(from_west, LANES - HALO - f * HALO, 1)
    return jnp.where(lane < HALO, east, jnp.where(lane >= LANES - HALO, west, 0.0))


def strips_kernel(ca, vo, co, to_west, to_east):
    fields = [ca.at[0], ca.at[1], vo.at[0], vo.at[1], co]
    left, right = side_strips([(f[:, :LANES], f[:, LANES:]) for f in fields])
    to_west[...] = left
    to_east[...] = right


def ends_kernel(ca, vo, co, from_east, from_west, to_north, to_south):
    fields = [ca.at[0], ca.at[1], vo.at[0], vo.at[1], co]
    for f, ref in enumerate(fields):
        for rows, out in ((slice(0, HALO), to_north), (slice(128 - HALO, 128), to_south)):
            out[f, :, : 2 * LANES] = ref[rows, :]
            out[f, :, 2 * LANES :] = side_tile(from_east[rows, :], from_west[rows, :], f)


def ends2_kernel(force, from_east, from_west, to_north, to_south):
    for f in range(2):
        for rows, out in ((slice(0, HALO), to_north), (slice(128 - HALO, 128), to_south)):
            out[f, :, : 2 * LANES] = force[f, rows, :]
            out[f, :, 2 * LANES :] = side_tile(from_east[rows, :], from_west[rows, :], f)


def pack_kernel(count, target, row, info, fluid, out):
    slots = fluid.shape[0]
    t_row = target[...]
    order = iota((1, slots), 1)
    used = order < count[0]
    eye = iota((slots, slots), 0) == iota((slots, slots), 1)
    t_col = jnp.sum(jnp.where(eye, t_row, 0), axis=1, keepdims=True)
    earlier = (
        (t_col == t_row)
        & (iota((slots, slots), 0) < count[0])
        & (iota((slots, slots), 0) < iota((slots, slots), 1))
    )
    rank = jnp.sum(jnp.where(earlier, 1, 0), axis=0, keepdims=True)
    place = jnp.where(used, rank * 128 + t_row, -1)
    pick = iota((256, slots), 0) == place
    tags = jnp.sum(jnp.where(pick, row[...] + 1, 0), axis=1, keepdims=True).astype(jnp.float32)
    moved = jnp.dot(
        pick.astype(jnp.float32), fluid[...], precision=HIGH, preferred_element_type=jnp.float32
    )
    out[:, :512] = moved[:128]
    out[:, 512:1024] = moved[128:]
    lane = iota((128, LANES), 1)
    tail = jnp.where(lane == 0, tags[:128], jnp.where(lane == 1, tags[128:], info[...]))
    out[:, 1024:] = tail


def force_kernel(got, force, to_west, to_east):
    tail = got[:, 1024:]
    line = iota((128, 128), 1).astype(jnp.float32) + 1.0
    dims = (((0,), (0,)), ((), ()))
    total = lax.dot_general(
        (tail[:, 0:1] == line).astype(jnp.float32),
        got[:, :512],
        dims,
        precision=HIGH,
        preferred_element_type=jnp.float32,
    ) + lax.dot_general(
        (tail[:, 1:2] == line).astype(jnp.float32),
        got[:, 512:1024],
        dims,
        precision=HIGH,
        preferred_element_type=jnp.float32,
    )
    shear = total[:, :256]
    agonist = total[:, 256:]
    stress = shear * shear / (1.0 + shear * shear)
    stimulus = 0.5 + 0.5 * jnp.tanh(0.5 * agonist)
    a_s = 0.1 * stimulus
    a_e = 0.02 + 0.15 * stress + 0.04 * stimulus
    force[0] = a_s
    force[1] = a_e
    left, right = side_strips([(a[:, :LANES], a[:, LANES:]) for a in (a_s, a_e)])
    to_west[...] = left
    to_east[...] = right


def extract(radius, refs, cells, table, tmp, out):
    side = 2 * radius + 1
    deep = -(-side // 8) * 8
    lane = iota((deep, LANES), 1)
    for slot in range(8):
        cell = cells[slot]
        row = cell // 256 + TOP - radius
        col = cell % 256 - radius
        base = pl.multiple_of(row // 8 * 8, 8)
        up = row - base
        kept = jnp.zeros((deep, LANES), jnp.float32)
        for f, ref in enumerate(refs):
            window = ref[pl.ds(base, deep + 8), :]
            window = pltpu.roll(window, (deep + 8 - up) % (deep + 8), 0)[:deep]
            window = pltpu.roll(window, (2 * WIDE - col + f * side) % WIDE, 1)[:, :LANES]
            kept = jnp.where((lane >= f * side) & (lane < (f + 1) * side), window, kept)
        tmp[slot * deep : (slot + 1) * deep, :] = kept
    pieces = tmp[: 8 * deep, :]
    width = table.shape[1]
    pick = (iota((LANES, width), 0) == table[0:1, :]).astype(jnp.float32)
    spread_out = jnp.dot(pieces, pick, precision=HIGH, preferred_element_type=jnp.float32)
    mine = iota((8 * deep, width), 0) == table[1:2, :]
    line = jnp.sum(jnp.where(mine, spread_out, 0.0), axis=0, keepdims=True)
    out[...] = jnp.broadcast_to(line, (128, width))


def build_ext(dst, centre, side, north, south):
    dst[TOP : TOP + 128, : 2 * LANES] = centre
    dst[TOP : TOP + 128, 2 * LANES :] = side
    dst[TOP - HALO : TOP, :] = north
    dst[TOP + 128 : TOP + 128 + HALO, :] = south
    clear_ends(dst)


def clear_ends(dst):
    dst[: TOP - HALO, :] = jnp.zeros((TOP - HALO, WIDE), jnp.float32)
    dst[TOP + 128 + HALO :, :] = jnp.zeros((EXT - TOP - 128 - HALO, WIDE), jnp.float32)


def first_patch_kernel(
    cells, ca, vo, co, from_east, from_west, from_north, from_south, force, table, ext, out, tmp
):
    fields = [ca.at[0], ca.at[1], vo.at[0], vo.at[1], co]
    for f, ref in enumerate(fields):
        scale = 0.05 if f == 4 else 1.0
        build_ext(
            ext.at[f],
            ref[...] * scale,
            side_tile(from_east[...], from_west[...], f) * scale,
            from_north[f] * scale,
            from_south[f] * scale,
        )
    tmp_force = ext.at[5]
    tmp_force[...] = jnp.zeros((EXT, WIDE), jnp.float32)
    tmp_force[TOP : TOP + 128, : 2 * LANES] = force[0]
    refs = [ext.at[2], ext.at[0], ext.at[3], ext.at[4], ext.at[1], ext.at[5]]
    extract(2, refs, cells, table, tmp, out)


def port_places(tail_t):
    rows = tail_t[8:16].astype(jnp.int32)
    cols = tail_t[16:24].astype(jnp.int32)
    partner = tail_t[24:32].astype(jnp.int32)
    return rows, cols, partner


def port_sim(radius, got, codes, rows, cols, partner):
    plan = patch_plan(radius)
    fields = [{} for _ in range(7)]
    for index, (field, cell) in enumerate(plan):
        fields[field][cell] = got[index * 8 : index * 8 + 8]
    v, s, u, spread, e, a_s, a_e = fields
    device = partner // 8
    slot = partner % 8

    def near(f, cell):
        a, b = cell
        left = jnp.where(cols == -b, f[cell], f[(a, b - 1)])
        right = jnp.where(cols == 4095 - b, f[cell], f[(a, b + 1)])
        return f[(a - 1, b)] + f[(a + 1, b)] + left + right

    gains = []
    for step in range(radius + 1):
        here = v[(0, 0)]
        theirs = jnp.zeros_like(here)
        for k in range(8):
            line = jnp.broadcast_to(here[k : k + 1], here.shape)
            theirs = jnp.where(slot == k, jnp.take_along_axis(line, device, axis=1), theirs)
        gain = 0.2 * (theirs - here)
        gains.append(gain)
        reach = radius - 1 - step
        if reach < 0:
            break
        cells = diamond(reach)
        added = {c: jnp.zeros_like(gain) for c in cells}
        index = 0
        for k in range(8):
            turned = pltpu.roll(gain, k, 0) if k else gain
            for shift in NEAR_LANES:
                moved = pltpu.roll(turned, (-shift) % LANES, 1) if shift else turned
                code = codes[index]
                index += 1
                for c in cells:
                    key = (c[0] * ROW_KEY + c[1]) & KEY_MASK
                    added[c] = added[c] + jnp.where(code == key, moved, 0.0)
        new_v = {}
        for c in cells:
            new_v[c] = v_step(s[c], v[c], u[c], near(v, c), spread[c]) + added[c]
        new_s, new_u, new_e = {}, {}, {}
        for c in diamond(reach - 1):
            new_s[c] = s_step(s[c], e[c], v[c], near(s, c), spread[c], a_s[c])
            new_u[c] = u_step(e[c], v[c], u[c], near(u, c), spread[c])
        for c in diamond(reach - 2):
            new_e[c] = e_step(s[c], e[c], near(e, c), spread[c], a_e[c])
        v, s, u, e = new_v, new_s, new_u, new_e
    return gains


def s_step(s, e, v, near, spread, a_s):
    return (
        s
        + (0.04 * jnp.tanh(v + 0.3) + 0.04)
        + a_s
        - 0.12 * s / (s + 0.5)
        + 0.03 * (e - s)
        + spread * (near - 4.0 * s)
    )


def e_step(s, e, near, spread, a_e):
    return e + a_e - 0.09 * e + 0.03 * (s - e) + spread * (near - 4.0 * e)


def v_step(s, v, u, near, spread):
    return (
        v
        - 0.1 * (v + 0.5)
        - 0.15 * s / (s + 1.0) * (v + 1.2)
        + 0.04 * (u - v)
        + spread * (near - 4.0 * v)
    )


def u_step(e, v, u, near, spread):
    return (
        u
        - 0.08 * (u + 0.4)
        - 0.1 * e / (e + 1.0) * (u + 1.2)
        + 0.04 * (v - u)
        + spread * (near - 4.0 * u)
    )


def make_codes(rows, cols, codes):
    key = rows * ROW_KEY + cols
    index = 0
    for k in range(8):
        turned = pltpu.roll(key, k, 0) if k else key
        for shift in NEAR_LANES:
            moved = pltpu.roll(turned, (-shift) % LANES, 1) if shift else turned
            codes[index] = (moved - key) & KEY_MASK
            index += 1


def my_column(value, lane_of):
    tiles = []
    lane = iota((8, LANES), 1)
    for shift in NEAR_LANES:
        at = (lane_of + shift) & (LANES - 1)
        tiles.append(jnp.sum(jnp.where(lane == at, value, 0.0), axis=1, keepdims=True))
    tiles.append(jnp.zeros((128 - 8 * len(tiles), 1), jnp.float32))
    return jnp.concatenate(tiles, axis=0)


def injections(place, rows, cols, gains, inject):
    i_circ = place[0]
    i_axial = place[1]
    lane_of = i_circ * 16 + i_axial
    row = my_column(rows.astype(jnp.float32), lane_of).astype(jnp.int32)
    col = my_column(cols.astype(jnp.float32), lane_of).astype(jnp.int32)
    row = ((row - i_circ * 128 + HALO) & 1023) + (TOP - HALO)
    col = col - i_axial * 256
    ok = (iota((128, 1), 0) < 72) & (col >= -HALO) & (col < 256 + HALO)
    col = jnp.where(ok, jnp.where(col < 0, col + WIDE, col), -1)
    in_row = jnp.where(row == iota((128, 256), 1), 1.0, 0.0)
    in_row = jnp.transpose(in_row)[:EXT]
    in_col = col == iota((128, WIDE), 1)
    for k, gain in enumerate(gains):
        line = jnp.where(in_col, my_column(gain, lane_of), 0.0)
        inject[k] = jnp.dot(in_row, line, precision=HIGH, preferred_element_type=jnp.float32)


def run_steps(steps, state, coef, inject, place):
    lane = iota((8, WIDE), 1)
    first = (lane == 0) & (place[1] == 0)
    last = (lane == 255) & (place[1] == 15)

    for f in range(4):
        clear_ends(state.at[1, f])

    def one(k, carry):
        now = lax.rem(k, 2)
        later = 1 - now
        for tile in range(1, EXT // 8 - 1):
            at = slice(tile * 8, tile * 8 + 8)
            mid, near = [], []
            for f in range(4):
                x = state[now, f, at, :]
                up = state[now, f, tile * 8 - 1 : tile * 8 + 7, :]
                down = state[now, f, tile * 8 + 1 : tile * 8 + 9, :]
                left = jnp.where(first, x, pltpu.roll(x, 1, 1))
                right = jnp.where(last, x, pltpu.roll(x, WIDE - 1, 1))
                mid.append(x)
                near.append(up + down + left + right)
            s, e, v, u = mid
            spread = coef[0][at, :]
            state[later, 0, at, :] = s_step(s, e, v, near[0], spread, coef[1][at, :])
            state[later, 1, at, :] = e_step(s, e, near[1], spread, coef[2][at, :])
            state[later, 2, at, :] = v_step(s, v, u, near[2], spread) + inject[k, at, :]
            state[later, 3, at, :] = u_step(e, v, u, near[3], spread)
        return carry

    lax.fori_loop(0, steps, one, 0)


def first_steps_kernel(
    place, cells, ext, force, from_east, from_west, from_north, from_south, got, tail, table,
    kept, out, state, codes, inject, tmp
):
    rows, cols, partner = port_places(jnp.transpose(tail[...]))
    make_codes(rows, cols, codes)
    gains = port_sim(2, jnp.transpose(got[...]), codes, rows, cols, partner)
    injections(place, rows, cols, gains, inject)
    for f in range(4):
        state[0, f] = ext[f]
    kept[4] = ext[4]
    for f in range(2):
        build_ext(
            kept.at[5 + f],
            force[f],
            side_tile(from_east[...], from_west[...], f),
            from_north[f],
            from_south[f],
        )
    run_steps(3, state, (kept.at[4], kept.at[5], kept.at[6]), inject, place)
    for f in range(4):
        kept[f] = state[1, f]
    refs = [kept.at[f] for f in (2, 0, 3, 4, 1, 5, 6)]
    extract(4, refs, cells, table, tmp, out)


def last_steps_kernel(place, kept, got, tail, ca_out, vo_out, state, codes, inject):
    rows, cols, partner = port_places(jnp.transpose(tail[...]))
    make_codes(rows, cols, codes)
    gains = port_sim(4, jnp.transpose(got[...]), codes, rows, cols, partner)
    injections(place, rows, cols, gains, inject)
    for f in range(4):
        state[0, f] = kept[f]
    run_steps(5, state, (kept.at[4], kept.at[5], kept.at[6]), inject, place)
    for f in range(2):
        ca_out[f] = state[1, f, TOP : TOP + 128, : 2 * LANES]
        vo_out[f] = state[1, f + 2, TOP : TOP + 128, : 2 * LANES]


def shifted(value, axis, step, periodic):
    count = lax.axis_size(axis)
    pairs = [(i, i + step) for i in range(count)]
    if periodic:
        pairs = [(i, j % count) for i, j in pairs]
    return lax.ppermute(value, axis, [(i, j) for i, j in pairs if 0 <= j < count])


def swap_axial(to_west, to_east):
    return shifted(to_west, "axial", -1, False), shifted(to_east, "axial", 1, False)


def swap_circ(to_north, to_south):
    return shifted(to_south, "circ", 1, True), shifted(to_north, "circ", -1, True)


def to_all(value):
    return lax.all_to_all(value, AXES, 0, 0, tiled=True)


def local(ca, vo, co, fluid, target, row, count, cells, partner):
    i_circ = lax.axis_index("circ")
    i_axial = lax.axis_index("axial")
    place = jnp.stack([i_circ, i_axial]).astype(jnp.int32)
    tables = [jnp.asarray(patch_tables(r)) for r in (2, 4)]
    widths = [t.shape[1] for t in tables]

    to_west, to_east = call(strips_kernel, [(128, LANES)] * 2, [VMEM] * 3, "strips")(ca, vo, co)
    from_east, from_west = swap_axial(to_west, to_east)

    info = jnp.concatenate(
        [
            jnp.zeros((8,), jnp.float32),
            (i_circ * 128 + cells // 256).astype(jnp.float32),
            (i_axial * 256 + cells % 256).astype(jnp.float32),
            partner.astype(jnp.float32),
            jnp.zeros((LANES - 32,), jnp.float32),
        ]
    )[None]
    (packed,) = call(pack_kernel, [(128, 1152)], [SMEM] + [VMEM] * 4, "pack")(
        count, target.reshape(1, -1), row.reshape(1, -1), info, fluid.reshape(192, 512)
    )
    to_north, to_south = call(ends_kernel, [(5, HALO, WIDE)] * 2, [VMEM] * 5, "ends")(
        ca, vo, co, from_east, from_west
    )
    from_north, from_south = swap_circ(to_north, to_south)
    received = to_all(packed)
    tail = received[:, 1024:]

    force, f_west, f_east = call(
        force_kernel, [(2, 128, 256), (128, LANES), (128, LANES)], [VMEM], "force"
    )(received)
    f_from_east, f_from_west = swap_axial(f_west, f_east)
    ext, patches = call(
        first_patch_kernel,
        [(6, EXT, WIDE), (128, widths[0])],
        [SMEM] + [VMEM] * 9,
        "first_patch",
        [pltpu.VMEM((128, LANES), jnp.float32)],
    )(cells, ca, vo, co, from_east, from_west, from_north, from_south, force, tables[0])
    f_north, f_south = call(ends2_kernel, [(2, HALO, WIDE)] * 2, [VMEM] * 3, "ends2")(
        force, f_from_east, f_from_west
    )
    f_from_north, f_from_south = swap_circ(f_north, f_south)
    got = to_all(patches)

    state = pltpu.VMEM((2, 4, EXT, WIDE), jnp.float32)
    codes = pltpu.VMEM((72, 8, LANES), jnp.int32)
    kept, patches = call(
        first_steps_kernel,
        [(7, EXT, WIDE), (128, widths[1])],
        [SMEM] * 2 + [VMEM] * 9,
        "first_steps",
        [state, codes, pltpu.VMEM((3, EXT, WIDE), jnp.float32), pltpu.VMEM((128, LANES), jnp.float32)],
    )(
        place, cells, ext, force, f_from_east, f_from_west, f_from_north, f_from_south, got, tail,
        tables[1],
    )
    got = to_all(patches)
    return call(
        last_steps_kernel,
        [(2, 128, 256)] * 2,
        [SMEM] + [VMEM] * 3,
        "last_steps",
        [state, codes, pltpu.VMEM((5, EXT, WIDE), jnp.float32)],
    )(place, kept, got, tail)


def solution(mesh):
    return jax.shard_map(
        local,
        mesh=mesh,
        in_specs=(
            P(None, "circ", "axial"),
            P(None, "circ", "axial"),
            P("circ", "axial"),
            P(AXES, None, None),
            P(AXES, None),
            P(AXES),
            P(AXES),
            P(AXES),
            P(AXES),
        ),
        out_specs=(P(None, "circ", "axial"), P(None, "circ", "axial")),
        check_vma=False,
    )
```

```python
import functools

import jax
import jax.numpy as jnp
import numpy as np
from jax import lax
from jax.experimental import pallas as pl
from jax.experimental.pallas import tpu as pltpu
from jax.sharding import PartitionSpec as P

AXES = ("circ", "axial")
HALO = 8
LANES = 128
WIDE = 384
RADIUS = 2
SIDE = 5
BLOCK = 9
TOP = 16
EXT = 160
NEAR_LANES = (0, 1, -1, 16, -16, 15, -15, 17, -17)
ROW_KEY = 8192
KEY_MASK = 1024 * ROW_KEY - 1
VMEM = pl.BlockSpec(memory_space=pltpu.VMEM)
SMEM = pl.BlockSpec(memory_space=pltpu.SMEM)


def diamond(radius):
    if radius < 0:
        return []
    span = range(-radius, radius + 1)
    return [(a, b) for a in span for b in span if abs(a) + abs(b) <= radius]


def patch_plan():
    radii = (2, 1, 1, 1, 0, 0, 0)
    return [(field, cell) for field, r in enumerate(radii) for cell in diamond(r)]


def patch_table():
    table = np.full((8, 2 * LANES), -1, np.int32)
    for index, (field, (a, b)) in enumerate(patch_plan()):
        for slot in range(8):
            at = index * 8 + slot
            table[0, at] = field * SIDE + b + RADIUS
            table[1, at] = slot * 8 + a + RADIUS
    return table


def iota(shape, dim):
    return lax.broadcasted_iota(jnp.int32, shape, dim)


def call(kernel, outs, ins, name, scratch=()):
    return pl.pallas_call(
        kernel,
        out_shape=tuple(jax.ShapeDtypeStruct(s, jnp.float32) for s in outs),
        in_specs=ins,
        out_specs=tuple(VMEM for _ in outs),
        scratch_shapes=list(scratch),
        name=name,
    )


def side_strips(tiles):
    rows = tiles[0][0].shape[0]
    lane = iota((rows, LANES), 1)
    left = jnp.zeros((rows, LANES), jnp.float32)
    right = left
    for f, (first, last) in enumerate(tiles):
        mine = (lane >= f * HALO) & (lane < (f + 1) * HALO)
        left = jnp.where(mine, pltpu.roll(first, f * HALO, 1) if f else first, left)
        right = jnp.where(mine, pltpu.roll(last, f * HALO + HALO, 1), right)
    return left, right


def side_tile(from_east, from_west, f):
    lane = iota(from_east.shape, 1)
    east = pltpu.roll(from_east, (LANES - f * HALO) % LANES, 1) if f else from_east
    west = pltpu.roll(from_west, LANES - HALO - f * HALO, 1)
    return jnp.where(lane < HALO, east, jnp.where(lane >= LANES - HALO, west, 0.0))


def exact_pick(pick, x):
    pick = jnp.where(pick, 1.0, 0.0).astype(jnp.bfloat16)
    high = x.astype(jnp.bfloat16)
    rest = x - high.astype(jnp.float32)
    middle = rest.astype(jnp.bfloat16)
    low = (rest - middle.astype(jnp.float32)).astype(jnp.bfloat16)
    total = jnp.dot(pick, low, preferred_element_type=jnp.float32)
    total = total + jnp.dot(pick, middle, preferred_element_type=jnp.float32)
    return total + jnp.dot(pick, high, preferred_element_type=jnp.float32)


def lanes_to(x, source, target, count):
    lane = iota(x.shape, 1)
    turned = pltpu.roll(x, (target - source) % LANES, 1) if target != source else x
    return jnp.where((lane >= target) & (lane < target + count), turned, 0.0)


def pack_kernel(
    count, cells, partner, target, row, fluid, ca, vo, co, packed, to_west, to_east
):
    i_circ = lax.axis_index("circ")
    i_axial = lax.axis_index("axial")
    fields = [ca.at[0], ca.at[1], vo.at[0], vo.at[1], co]
    left, right = side_strips([(f[:, :LANES], f[:, LANES:]) for f in fields])
    to_west[...] = left
    to_east[...] = right
    slots = fluid.shape[0]
    t_row = target[...]
    order = iota((1, slots), 1)
    used = order < count[0]
    eye = iota((slots, slots), 0) == iota((slots, slots), 1)
    t_col = jnp.sum(jnp.where(eye, t_row, 0), axis=1, keepdims=True)
    earlier = (
        (t_col == t_row)
        & (iota((slots, slots), 0) < count[0])
        & (iota((slots, slots), 0) < iota((slots, slots), 1))
    )
    rank = jnp.sum(jnp.where(earlier, 1, 0), axis=0, keepdims=True)
    place = jnp.where(used, rank * 128 + t_row, -1)
    pick = iota((256, slots), 0) == place
    tags = jnp.sum(jnp.where(pick, row[...] + 1, 0), axis=1, keepdims=True).astype(jnp.float32)
    tags0, tags1 = tags[:128], tags[128:]
    moved = exact_pick(pick, fluid[...])
    for half in range(2):
        for part in range(4):
            packed[pl.ds(half * 4 + part, 128, stride=BLOCK), :] = moved[
                half * 128 : half * 128 + 128, part * LANES : part * LANES + LANES
            ]
    lane = iota((128, LANES), 1)
    tail = jnp.where(lane == 0, tags0, jnp.where(lane == 1, tags1, 0.0))
    for slot in range(8):
        cell = cells[slot]
        for base, value in (
            (8, i_circ * 128 + cell // 256),
            (16, i_axial * 256 + cell % 256),
            (24, partner[slot]),
        ):
            tail = jnp.where(lane == base + slot, value.astype(jnp.float32), tail)
    east = jnp.where(lane == 2, tags0, jnp.where(lane == 3, tags1, 0.0))
    west = jnp.where(lane == 4, tags0, jnp.where(lane == 5, tags1, 0.0))
    for half in range(2):
        rows = moved[half * 128 : half * 128 + 128]
        for k in range(2):
            first = rows[:, 2 * k * LANES : (2 * k + 1) * LANES]
            last = rows[:, (2 * k + 1) * LANES : (2 * k + 2) * LANES]
            east = east + lanes_to(first, 0, 32 + half * 16 + k * HALO, HALO)
            west = west + lanes_to(last, LANES - HALO, 64 + half * 16 + k * HALO, HALO)
    tail = tail + pltpu.roll(east, 127, 0) + pltpu.roll(west, 1, 0)
    packed[pl.ds(8, 128, stride=BLOCK), :] = tail


def force_kernel(got, ca, vo, co, from_east, from_west, force, ports, to_north, to_south):
    tail = got[pl.ds(8, 128, stride=BLOCK), :]
    tail_t = jnp.transpose(tail)
    ports[...] = tail_t[8:32]
    line = iota((128, 128), 0).astype(jnp.float32) + 1.0

    def picked(k, x):
        return exact_pick(tail_t[k : k + 1] == line, x)

    halves = []
    for half in range(2):
        parts = [got[pl.ds(half * 4 + part, 128, stride=BLOCK), :] for part in range(4)]
        halves.append(picked(half, jnp.concatenate(parts, axis=1)))
    total = halves[0] + halves[1]
    east = picked(2, tail) + pltpu.roll(picked(3, tail), LANES - 16, 1)
    west = picked(4, tail) + pltpu.roll(picked(5, tail), LANES - 16, 1)
    sides = [
        lanes_to(east, 32 + k * HALO, 0, HALO) + lanes_to(west, 64 + k * HALO, LANES - HALO, HALO)
        for k in range(2)
    ]
    shear = jnp.concatenate([total[:, :256], sides[0]], axis=1)
    agonist = jnp.concatenate([total[:, 256:], sides[1]], axis=1)
    stress = shear * shear / (1.0 + shear * shear)
    stimulus = 0.5 + 0.5 * jnp.tanh(0.5 * agonist)
    a_s = 0.1 * stimulus
    a_e = 0.02 + 0.15 * stress + 0.04 * stimulus
    force[0] = a_s
    force[1] = a_e
    fields = [ca.at[0], ca.at[1], vo.at[0], vo.at[1], co]
    for rows, out in ((slice(0, HALO), to_north), (slice(128 - HALO, 128), to_south)):
        for f, ref in enumerate(fields):
            out[f, :, : 2 * LANES] = ref[rows, :]
            out[f, :, 2 * LANES :] = side_tile(from_east[rows, :], from_west[rows, :], f)
        out[5] = a_s[rows]
        out[6] = a_e[rows]


def extract(refs, cells, table, tmp, out):
    lane = iota((8, LANES), 1)
    for slot in range(8):
        cell = cells[slot]
        row = cell // 256 + TOP - RADIUS
        col = cell % 256 - RADIUS
        base = pl.multiple_of(row // 8 * 8, 8)
        up = row - base
        kept = jnp.zeros((8, LANES), jnp.float32)
        for f, ref in enumerate(refs):
            window = ref[pl.ds(base, 16), :]
            window = pltpu.roll(window, 16 - up, 0)[:8]
            window = pltpu.roll(window, (2 * WIDE - col + f * SIDE) % WIDE, 1)[:, :LANES]
            kept = jnp.where((lane >= f * SIDE) & (lane < (f + 1) * SIDE), window, kept)
        tmp[slot * 8 : slot * 8 + 8, :] = kept
    width = 2 * LANES
    pieces = exact_take(tmp[...], iota((LANES, width), 0) == table[0:1, :])
    mine = iota((64, width), 0) == table[1:2, :]
    line = jnp.sum(jnp.where(mine, pieces, 0.0), axis=0, keepdims=True)
    for k in range(2):
        out[pl.ds(k, 128, stride=2), :] = jnp.broadcast_to(
            line[:, k * LANES : (k + 1) * LANES], (128, LANES)
        )


def exact_take(x, pick):
    pick = jnp.where(pick, 1.0, 0.0).astype(jnp.bfloat16)
    high = x.astype(jnp.bfloat16)
    rest = x - high.astype(jnp.float32)
    middle = rest.astype(jnp.bfloat16)
    low = (rest - middle.astype(jnp.float32)).astype(jnp.bfloat16)
    total = jnp.dot(low, pick, preferred_element_type=jnp.float32)
    total = total + jnp.dot(middle, pick, preferred_element_type=jnp.float32)
    return total + jnp.dot(high, pick, preferred_element_type=jnp.float32)


def build_ext(dst, centre, side, north, south):
    dst[TOP : TOP + 128, : 2 * LANES] = centre
    dst[TOP : TOP + 128, 2 * LANES :] = side
    dst[TOP - HALO : TOP, :] = north
    dst[TOP + 128 : TOP + 128 + HALO, :] = south
    clear_ends(dst)


def clear_ends(dst):
    dst[: TOP - HALO, :] = jnp.zeros((TOP - HALO, WIDE), jnp.float32)
    dst[TOP + 128 + HALO :, :] = jnp.zeros((EXT - TOP - 128 - HALO, WIDE), jnp.float32)


def first_patch_kernel(
    cells, ca, vo, co, from_east, from_west, from_north, from_south, force, table,
    kept, out, start, tmp
):
    fields = [ca.at[0], ca.at[1], vo.at[0], vo.at[1], co]
    for f, ref in enumerate(fields):
        scale = 0.05 if f == 4 else 1.0
        build_ext(
            start.at[f] if f < 4 else kept.at[4],
            ref[...] * scale,
            side_tile(from_east[...], from_west[...], f) * scale,
            from_north[f] * scale,
            from_south[f] * scale,
        )
        if f < 4:
            clear_ends(kept.at[f])
    for f in range(2):
        build_ext(
            kept.at[5 + f], force[f, :, :256], force[f, :, 256:], from_north[5 + f], from_south[5 + f]
        )
    one_step(
        [start.at[f] for f in range(4)], [kept.at[f] for f in range(4)], coefs(kept), None
    )
    take_patches(kept, kept, start.at[2], cells, table, tmp, out)


def coefs(kept):
    return [kept.at[f] for f in (4, 5, 6)]


def take_patches(after, coef, before_v, cells, table, tmp, out):
    refs = [after.at[2], after.at[0], after.at[3], coef.at[4], after.at[1], coef.at[5], before_v]
    extract(refs, cells, table, tmp, out)


def port_places(ports):
    return [ports[k * 8 : k * 8 + 8, :].astype(jnp.int32) for k in range(3)]


def port_sim(got, codes, rows, cols, partner):
    got_t = [jnp.transpose(got[pl.ds(k, 128, stride=2), :]) for k in range(2)]
    fields = [{} for _ in range(7)]
    for index, (field, cell) in enumerate(patch_plan()):
        at = index * 8 % LANES
        fields[field][cell] = got_t[index * 8 // LANES][at : at + 8]
    v, s, u, spread, e, a_s, before = fields
    device = partner // 8
    slot = partner % 8

    def near(f, cell):
        a, b = cell
        left = jnp.where(cols == -b, f[cell], f[(a, b - 1)])
        right = jnp.where(cols == 4095 - b, f[cell], f[(a, b + 1)])
        return f[(a - 1, b)] + f[(a + 1, b)] + left + right

    def gain_of(here):
        theirs = jnp.zeros_like(here)
        for k in range(8):
            line = jnp.broadcast_to(here[k : k + 1], here.shape)
            theirs = jnp.where(slot == k, jnp.take_along_axis(line, device, axis=1), theirs)
        return 0.2 * (theirs - here)

    def add_gain(f, gain, reach):
        added = dict(f)
        index = 0
        for k in range(8):
            turned = pltpu.roll(gain, k, 0) if k else gain
            for shift in NEAR_LANES:
                moved = pltpu.roll(turned, (-shift) % LANES, 1) if shift else turned
                code = codes[index]
                index += 1
                for c in diamond(reach):
                    key = (c[0] * ROW_KEY + c[1]) & KEY_MASK
                    added[c] = added[c] + jnp.where(code == key, moved, 0.0)
        return added

    gains = [gain_of(before[(0, 0)])]
    v = add_gain(v, gains[0], RADIUS)
    for step in range(RADIUS + 1):
        gains.append(gain_of(v[(0, 0)]))
        reach = RADIUS - 1 - step
        if reach < 0:
            break
        parts = {c: reciprocals(s[c], e.get(c)) for c in diamond(reach)}
        new_v = {}
        for c in diamond(reach):
            new_v[c] = v_step(parts[c], v[c], u[c], near(v, c), spread[c])
        new_s, new_u = {}, {}
        for c in diamond(reach - 1):
            new_s[c] = s_step(parts[c], s[c], e[c], v[c], near(s, c), spread[c], a_s[c])
            new_u[c] = u_step(parts[c], v[c], u[c], near(u, c), spread[c])
        v = add_gain(new_v, gains[-1], reach)
        s, u = new_s, new_u
    return gains


def reciprocals(s, e):
    half, whole = s + 0.5, s + 1.0
    both = half * whole
    if e is None:
        inv = 1.0 / both
        return inv * whole, inv * half, None
    end = e + 1.0
    inv = 1.0 / (both * end)
    rest = inv * end
    return rest * whole, rest * half, inv * both


def s_step(parts, s, e, v, near, spread, a_s):
    return (
        s * (0.97 - 4.0 * spread)
        + 0.03 * e
        + (a_s - 0.08)
        + 0.04 * jnp.tanh(v + 0.3)
        + 0.06 * parts[0]
        + spread * near
    )


def e_step(s, e, near, spread, a_e):
    return e * (0.88 - 4.0 * spread) + 0.03 * s + a_e + spread * near


def v_step(parts, v, u, near, spread):
    return (
        v * (0.71 - 4.0 * spread + 0.15 * parts[1])
        + 0.18 * parts[1]
        - 0.23
        + 0.04 * u
        + spread * near
    )


def u_step(parts, v, u, near, spread):
    return (
        u * (0.78 - 4.0 * spread + 0.1 * parts[2])
        + 0.12 * parts[2]
        - 0.152
        + 0.04 * v
        + spread * near
    )


def make_codes(rows, cols, codes):
    key = rows * ROW_KEY + cols
    index = 0
    for k in range(8):
        turned = pltpu.roll(key, k, 0) if k else key
        for shift in NEAR_LANES:
            moved = pltpu.roll(turned, (-shift) % LANES, 1) if shift else turned
            codes[index] = (moved - key) & KEY_MASK
            index += 1


def my_column(value, lane_of):
    tiles = []
    lane = iota((8, LANES), 1)
    for shift in NEAR_LANES:
        at = (lane_of + shift) & (LANES - 1)
        tiles.append(jnp.sum(jnp.where(lane == at, value, 0.0), axis=1, keepdims=True))
    tiles.append(jnp.zeros((128 - 8 * len(tiles), 1), jnp.float32))
    return jnp.concatenate(tiles, axis=0)


def injections(rows, cols, gains, inject):
    i_circ = lax.axis_index("circ")
    i_axial = lax.axis_index("axial")
    lane_of = i_circ * 16 + i_axial
    row = my_column(rows.astype(jnp.float32), lane_of).astype(jnp.int32)
    col = my_column(cols.astype(jnp.float32), lane_of).astype(jnp.int32)
    row = ((row - i_circ * 128 + HALO) & 1023) + (TOP - HALO)
    col = col - i_axial * 256
    ok = (iota((128, 1), 0) < 72) & (col >= -HALO) & (col < 256 + HALO)
    col = jnp.where(ok, jnp.where(col < 0, col + WIDE, col), -1)
    in_row = jnp.where(row == iota((128, 256), 1), 1.0, 0.0)
    in_row = jnp.transpose(in_row)[:EXT] > 0.5
    in_col = col == iota((128, WIDE), 1)
    for k, gain in enumerate(gains):
        line = jnp.where(in_col, my_column(gain, lane_of), 0.0)
        inject[k] = exact_pick(in_row, line)


def one_step(now, later, coef, inject):
    lane = iota((8, WIDE), 1)
    i_axial = lax.axis_index("axial")
    first = (lane == 0) & (i_axial == 0)
    last = (lane == 255) & (i_axial == 15)
    for tile in range(1, EXT // 8 - 1):
        at = slice(tile * 8, tile * 8 + 8)
        mid, near = [], []
        for f in range(4):
            x = now[f][at, :]
            up = now[f][tile * 8 - 1 : tile * 8 + 7, :]
            down = now[f][tile * 8 + 1 : tile * 8 + 9, :]
            left = jnp.where(first, x, pltpu.roll(x, 1, 1))
            right = jnp.where(last, x, pltpu.roll(x, WIDE - 1, 1))
            mid.append(x)
            near.append(up + down + left + right)
        s, e, v, u = mid
        spread = coef[0][at, :]
        parts = reciprocals(s, e)
        new_v = v_step(parts, v, u, near[2], spread)
        later[0][at, :] = s_step(parts, s, e, v, near[0], spread, coef[1][at, :])
        later[1][at, :] = e_step(s, e, near[1], spread, coef[2][at, :])
        later[2][at, :] = new_v if inject is None else new_v + inject[at, :]
        later[3][at, :] = u_step(parts, v, u, near[3], spread)


def coupled_steps(kept, got, ports, state, codes, inject):
    rows, cols, partner = port_places(ports)
    make_codes(rows, cols, codes)
    gains = port_sim(got, codes, rows, cols, partner)
    injections(rows, cols, gains, inject)
    for f in range(4):
        state[0, f] = kept[f] + inject[0] if f == 2 else kept[f]
        clear_ends(state.at[1, f])

    def one(k, carry):
        now = lax.rem(k, 2)
        one_step(
            [state.at[now, f] for f in range(4)],
            [state.at[1 - now, f] for f in range(4)],
            coefs(kept),
            inject.at[k + 1],
        )
        return carry

    lax.fori_loop(0, 3, one, 0)


def first_steps_kernel(cells, kept, got, ports, table, ahead, out, state, codes, inject, tmp):
    coupled_steps(kept, got, ports, state, codes, inject)
    for f in range(4):
        clear_ends(ahead.at[f])
    one_step(
        [state.at[1, f] for f in range(4)], [ahead.at[f] for f in range(4)], coefs(kept), None
    )
    take_patches(ahead, kept, state.at[1, 2], cells, table, tmp, out)


def last_steps_kernel(kept, ahead, got, ports, ca_out, vo_out, state, codes, inject):
    both = [ahead.at[f] for f in range(4)] + [kept.at[f] for f in (4, 5, 6)]
    coupled_steps(Views(both), got, ports, state, codes, inject)
    for f in range(2):
        ca_out[f] = state[1, f, TOP : TOP + 128, : 2 * LANES]
        vo_out[f] = state[1, f + 2, TOP : TOP + 128, : 2 * LANES]


class Views:
    def __init__(self, refs):
        self.refs = refs
        self.at = refs

    def __getitem__(self, k):
        return self.refs[k][...]


def shifted(value, axis, step, periodic):
    count = lax.axis_size(axis)
    pairs = [(i, i + step) for i in range(count)]
    if periodic:
        pairs = [(i, j % count) for i, j in pairs]
    return lax.ppermute(value, axis, [(i, j) for i, j in pairs if 0 <= j < count])


def swap_axial(to_west, to_east):
    return shifted(to_west, "axial", -1, False), shifted(to_east, "axial", 1, False)


def swap_circ(to_north, to_south):
    return shifted(to_south, "circ", 1, True), shifted(to_north, "circ", -1, True)


def to_all(value):
    blocks = value.reshape(128, 1, -1)
    return lax.all_to_all(blocks, AXES, 0, 0, tiled=True).reshape(value.shape)


def local(ca, vo, co, fluid, target, row, count, cells, partner):
    table = jnp.asarray(patch_table())
    packed, to_west, to_east = call(
        pack_kernel,
        [(128 * BLOCK, LANES), (128, LANES), (128, LANES)],
        [SMEM] * 3 + [VMEM] * 6,
        "pack",
    )(
        count, cells, partner, target.reshape(1, -1), row.reshape(1, -1), fluid.reshape(192, 512),
        ca, vo, co,
    )
    from_east, from_west = swap_axial(to_west, to_east)
    received = to_all(packed)
    force, ports, to_north, to_south = call(
        force_kernel,
        [(2, 128, WIDE), (24, LANES), (7, HALO, WIDE), (7, HALO, WIDE)],
        [VMEM] * 6,
        "force",
    )(received, ca, vo, co, from_east, from_west)
    from_north, from_south = swap_circ(to_north, to_south)
    tmp = pltpu.VMEM((64, LANES), jnp.float32)
    kept, patches = call(
        first_patch_kernel,
        [(7, EXT, WIDE), (256, LANES)],
        [SMEM] + [VMEM] * 9,
        "first_patch",
        [pltpu.VMEM((4, EXT, WIDE), jnp.float32), tmp],
    )(cells, ca, vo, co, from_east, from_west, from_north, from_south, force, table)
    got = to_all(patches)
    scratch = [
        pltpu.VMEM((2, 4, EXT, WIDE), jnp.float32),
        pltpu.VMEM((72, 8, LANES), jnp.int32),
        pltpu.VMEM((4, EXT, WIDE), jnp.float32),
    ]
    ahead, patches = call(
        first_steps_kernel,
        [(4, EXT, WIDE), (256, LANES)],
        [SMEM] + [VMEM] * 4,
        "first_steps",
        scratch + [tmp],
    )(cells, kept, got, ports, table)
    got = to_all(patches)
    return call(last_steps_kernel, [(2, 128, 256)] * 2, [VMEM] * 4, "last_steps", scratch)(
        kept, ahead, got, ports
    )


def solution(mesh):
    return jax.shard_map(
        local,
        mesh=mesh,
        in_specs=(
            P(None, "circ", "axial"),
            P(None, "circ", "axial"),
            P("circ", "axial"),
            P(AXES, None, None),
            P(AXES, None),
            P(AXES),
            P(AXES),
            P(AXES),
            P(AXES),
        ),
        out_specs=(P(None, "circ", "axial"), P(None, "circ", "axial")),
        check_vma=False,
    )
```

```python
import functools

import jax
import jax.numpy as jnp
import numpy as np
from jax import lax
from jax.experimental import pallas as pl
from jax.experimental.pallas import tpu as pltpu
from jax.sharding import PartitionSpec as P

AXES = ("circ", "axial")
HALO = 8
LANES = 128
WIDE = 384
RADIUS = 2
SIDE = 5
BLOCK = 9
EXT = 144
STEP = 18
NEAR_PORTS = 80
NEAR_LANES = (0, 1, -1, 16, -16, 15, -15, 17, -17)
ROW_KEY = 8192
KEY_MASK = 1024 * ROW_KEY - 1
VMEM = pl.BlockSpec(memory_space=pltpu.VMEM)
SMEM = pl.BlockSpec(memory_space=pltpu.SMEM)


def diamond(radius):
    if radius < 0:
        return []
    span = range(-radius, radius + 1)
    return [(a, b) for a in span for b in span if abs(a) + abs(b) <= radius]


def patch_plan():
    radii = (2, 1, 1, 1, 0, 0, 0)
    return [(field, cell) for field, r in enumerate(radii) for cell in diamond(r)]


def patch_table():
    table = np.full((8, 2 * LANES), -1, np.int32)
    for index, (field, (a, b)) in enumerate(patch_plan()):
        for slot in range(8):
            at = index * 8 + slot
            table[0, at] = field * SIDE + b + RADIUS
            table[1, at] = slot * 8 + a + RADIUS
    return table


def iota(shape, dim):
    return lax.broadcasted_iota(jnp.int32, shape, dim)


HELD = pl.BlockSpec(memory_space=pltpu.VMEM)


def call(kernel, outs, ins, name, scratch=(), last=jnp.float32, place=pltpu.VMEM, room=20):
    types = [jnp.float32] * (len(outs) - 1) + [last]
    run = pl.pallas_call(
        kernel,
        out_shape=tuple(place(s, t) for s, t in zip(outs, types)),
        in_specs=ins,
        out_specs=tuple(VMEM for _ in outs),
        scratch_shapes=list(scratch),
        name=name,
        compiler_params=pltpu.CompilerParams(vmem_limit_bytes=room * 1024 * 1024),
    )

    def placed(*args):
        return run(
            *(
                pltpu.with_memory_space_constraint(x, pltpu.VMEM) if spec is HELD else x
                for x, spec in zip(args, ins)
            )
        )

    return placed


def side_strips(tiles):
    rows = tiles[0][0].shape[0]
    lane = iota((rows, LANES), 1)
    left = jnp.zeros((rows, LANES), jnp.float32)
    right = left
    for f, (first, last) in enumerate(tiles):
        mine = (lane >= f * HALO) & (lane < (f + 1) * HALO)
        left = jnp.where(mine, pltpu.roll(first, f * HALO, 1) if f else first, left)
        right = jnp.where(mine, pltpu.roll(last, f * HALO + HALO, 1), right)
    return left, right


def side_tile(from_east, from_west, f):
    lane = iota(from_east.shape, 1)
    east = pltpu.roll(from_east, (LANES - f * HALO) % LANES, 1) if f else from_east
    west = pltpu.roll(from_west, LANES - HALO - f * HALO, 1)
    return jnp.where(lane < HALO, east, jnp.where(lane >= LANES - HALO, west, 0.0))


def three_parts(x):
    high = x.astype(jnp.bfloat16)
    rest = x - high.astype(jnp.float32)
    middle = rest.astype(jnp.bfloat16)
    low = (rest - middle.astype(jnp.float32)).astype(jnp.bfloat16)
    return high, middle, low


def one_hot(pick):
    return jnp.where(pick, 1.0, 0.0).astype(jnp.bfloat16)


def dot(a, b):
    return jnp.dot(a, b, preferred_element_type=jnp.float32)


def exact_pick(pick, x):
    pick = one_hot(pick)
    high, middle, low = three_parts(x)
    return dot(pick, low) + dot(pick, middle) + dot(pick, high)


def all_fields(ca, vo, co):
    return [ca.at[0], ca.at[1], vo.at[0], vo.at[1], co]


def strips_kernel(ca, vo, co, to_west, to_east):
    left, right = side_strips([(f[:, :LANES], f[:, LANES:]) for f in all_fields(ca, vo, co)])
    to_west[...] = jnp.transpose(left)[: 5 * HALO]
    to_east[...] = jnp.transpose(right)[: 5 * HALO]


def sides_kernel(from_east, from_west, sides):
    blank = jnp.zeros((LANES - 5 * HALO, LANES), jnp.float32)
    east = jnp.transpose(jnp.concatenate([from_east[...], blank], axis=0))
    west = jnp.transpose(jnp.concatenate([from_west[...], blank], axis=0))
    for f in range(5):
        sides[f] = side_tile(east, west, f)


def lanes_to(x, source, target, count):
    lane = iota(x.shape, 1)
    turned = pltpu.roll(x, (target - source) % LANES, 1) if target != source else x
    return jnp.where((lane >= target) & (lane < target + count), turned, 0.0)


def pack_kernel(count, cells, partner, target, row, fluid, packed):
    i_circ = lax.axis_index("circ")
    i_axial = lax.axis_index("axial")
    slots = fluid.shape[0] // 4
    t_row = target[...]
    order = iota((1, slots), 1)
    used = order < count[0]
    eye = iota((slots, slots), 0) == iota((slots, slots), 1)
    t_col = jnp.sum(jnp.where(eye, t_row, 0), axis=1, keepdims=True)
    earlier = (
        (t_col == t_row)
        & (iota((slots, slots), 0) < count[0])
        & (iota((slots, slots), 0) < iota((slots, slots), 1))
    )
    rank = jnp.sum(jnp.where(earlier, 1, 0), axis=0, keepdims=True)
    place = jnp.where(used, rank * 128 + t_row, -1)
    pick = iota((256, slots), 0) == place
    tags = jnp.sum(jnp.where(pick, row[...] + 1, 0), axis=1, keepdims=True).astype(jnp.float32)
    tags0, tags1 = tags[:128], tags[128:]
    tiles = [fluid[pl.ds(c * 2 + k, slots, stride=4), :] for k in range(2) for c in range(2)]
    moved = exact_pick(pick, jnp.concatenate(tiles, axis=1))
    for half in range(2):
        for part in range(4):
            packed[pl.ds(half * 4 + part, 128, stride=BLOCK), :] = moved[
                half * 128 : half * 128 + 128, part * LANES : part * LANES + LANES
            ]
    lane = iota((128, LANES), 1)
    tail = jnp.where(lane == 0, tags0, jnp.where(lane == 1, tags1, 0.0))
    for slot in range(8):
        cell = cells[slot]
        for base, value in (
            (8, i_circ * 128 + cell // 256),
            (16, i_axial * 256 + cell % 256),
            (24, partner[slot]),
        ):
            tail = jnp.where(lane == base + slot, value.astype(jnp.float32), tail)
    east = jnp.where(lane == 2, tags0, jnp.where(lane == 3, tags1, 0.0))
    west = jnp.where(lane == 4, tags0, jnp.where(lane == 5, tags1, 0.0))
    for half in range(2):
        rows = moved[half * 128 : half * 128 + 128]
        for k in range(2):
            first = rows[:, 2 * k * LANES : (2 * k + 1) * LANES]
            last = rows[:, (2 * k + 1) * LANES : (2 * k + 2) * LANES]
            east = east + lanes_to(first, 0, 32 + half * 16 + k * HALO, HALO)
            west = west + lanes_to(last, LANES - HALO, 64 + half * 16 + k * HALO, HALO)
    tail = tail + pltpu.roll(east, 127, 0) + pltpu.roll(west, 1, 0)
    packed[pl.ds(8, 128, stride=BLOCK), :] = tail


def force_kernel(got, ca, vo, co, sides, force, ports, to_north, to_south):
    tail = got[pl.ds(8, 128, stride=BLOCK), :]
    tail_t = jnp.transpose(tail)
    ports[...] = tail_t[8:32]
    line = iota((128, 128), 0).astype(jnp.float32) + 1.0

    def pair(k):
        return jnp.concatenate([tail_t[k : k + 1] == line, tail_t[k + 1 : k + 2] == line], axis=1)

    blocks = [
        jnp.concatenate(
            [got[pl.ds(half * 4 + part, 128, stride=BLOCK), :] for half in range(2)], axis=0
        )
        for part in range(4)
    ]
    total = exact_pick(pair(0), jnp.concatenate(blocks, axis=1))
    both = jnp.concatenate([tail, pltpu.roll(tail, LANES - 16, 1)], axis=0)
    both = jnp.concatenate(three_parts(both), axis=1)
    east, west = dot(one_hot(pair(2)), both), dot(one_hot(pair(4)), both)
    east, west = [x[:, 256:] + x[:, 128:256] + x[:, :128] for x in (east, west)]
    for tile in range(3):
        if tile < 2:
            shear = total[:, tile * LANES : (tile + 1) * LANES]
            agonist = total[:, (tile + 2) * LANES : (tile + 3) * LANES]
        else:
            shear, agonist = [
                lanes_to(east, 32 + k * HALO, 0, HALO)
                + lanes_to(west, 64 + k * HALO, LANES - HALO, HALO)
                for k in range(2)
            ]
        stress = shear * shear / (1.0 + shear * shear)
        stimulus = 0.5 + 0.5 * jnp.tanh(0.5 * agonist)
        a_s = 0.1 * stimulus
        a_e = 0.02 + 0.15 * stress + 0.04 * stimulus
        for f, value in enumerate((a_s, a_e)):
            force[f, tile] = value
            to_north[5 + f, tile] = value[:HALO]
            to_south[5 + f, tile] = value[128 - HALO :]
    for f, ref in enumerate(all_fields(ca, vo, co)):
        for rows, out in ((slice(0, HALO), to_north), (slice(128 - HALO, 128), to_south)):
            out[f, 0] = ref[rows, :LANES]
            out[f, 1] = ref[rows, LANES:]
            out[f, 2] = sides[f, rows, :]


def extract(refs, cells, table, tmp, out):
    lane = iota((8, LANES), 1)
    long_lane = iota((16, LANES), 1)
    for slot in range(8):
        cell = cells[slot]
        row = cell // 256 + HALO - RADIUS
        col = lax.rem(cell % 256 - RADIUS + WIDE, WIDE)
        base = pl.multiple_of(row // 8 * 8, 8)
        turn = 16 - (row - base)
        tile = col // LANES
        other = lax.rem(tile + 1, 3)
        inside = col % LANES
        kept = jnp.zeros((8, LANES), jnp.float32)
        for f, ref in enumerate(refs):
            window = jnp.where(
                long_lane < inside, ref[other, pl.ds(base, 16), :], ref[tile, pl.ds(base, 16), :]
            )
            window = pltpu.roll(window, turn, 0)[:8]
            window = pltpu.roll(window, (2 * LANES - inside + f * SIDE) % LANES, 1)
            kept = jnp.where((lane >= f * SIDE) & (lane < (f + 1) * SIDE), window, kept)
        tmp[slot * 8 : slot * 8 + 8, :] = kept
    width = 2 * LANES
    at = iota((LANES, width), 0)
    wanted = table[0:1, :]
    pick = one_hot((at == wanted) | (at == wanted + 40) | (at == wanted + 80))
    high, middle, low = [x.astype(jnp.float32) for x in three_parts(tmp[...])]
    pieces = dot(
        (high + pltpu.roll(middle, 40, 1) + pltpu.roll(low, 80, 1)).astype(jnp.bfloat16), pick
    )
    mine = iota((64, width), 0) == table[1:2, :]
    line = jnp.sum(jnp.where(mine, pieces, 0.0), axis=0, keepdims=True)
    for k in range(2):
        out[pl.ds(k, 128, stride=2), :] = jnp.broadcast_to(
            line[:, k * LANES : (k + 1) * LANES], (128, LANES)
        )


def build_rows(dst, tiles, north, south):
    for tile in range(3):
        dst[tile, HALO : HALO + 128, :] = tiles[tile]
        dst[tile, :HALO, :] = north[tile]
        dst[tile, HALO + 128 :, :] = south[tile]


def rows_at(j):
    return pl.ds(j, 8, stride=STEP)


def mixed_at(j):
    return pl.ds(8 * j, 8)


def to_mixed(src, dst):
    for tile in range(3):
        for j in range(STEP):
            dst[tile, mixed_at(j), :] = src[tile, rows_at(j), :]


def tables_kernel(ports, in_row, in_col, codes):
    rows, cols, _ = port_places(ports)
    make_codes(rows, cols, codes)
    i_circ = lax.axis_index("circ")
    i_axial = lax.axis_index("axial")
    row = my_column(rows.astype(jnp.float32)).astype(jnp.int32)
    col = my_column(cols.astype(jnp.float32)).astype(jnp.int32)
    row = (row - i_circ * 128 + HALO) & 1023
    col = col - i_axial * 256
    ok = (iota((NEAR_PORTS, 1), 0) < 72) & (col >= -HALO) & (col < 256 + HALO) & (row < EXT)
    col = jnp.where(ok, jnp.where(col < 0, col + WIDE, col), -1)
    group = lax.shift_right_logical(row * 57, 10)
    place = jnp.where(ok, (row - group * STEP) * 8 + group, -1)
    in_col[...] = jnp.where(col == iota((NEAR_PORTS, WIDE), 1), 1.0, 0.0)
    place = jnp.concatenate([place, place, place, jnp.full((16, 1), -1, jnp.int32)], axis=0)
    in_row[...] = jnp.transpose(jnp.where(place == iota((256, 256), 1), 1.0, 0.0))[:EXT]


def first_patch_kernel(
    cells, ca, vo, co, sides, from_north, from_south, force, table,
    ahead, coef, spread, pulled, out, start, tmp,
):
    for f, ref in enumerate(all_fields(ca, vo, co)):
        scale = 0.05 if f == 4 else 1.0
        build_rows(
            start.at[f] if f < 4 else spread,
            [t * scale for t in (ref[:, :LANES], ref[:, LANES:], sides[f])],
            from_north[f] * scale,
            from_south[f] * scale,
        )
    for f in range(2):
        build_rows(
            pulled if f == 0 else start.at[4],
            [force[f, tile] for tile in range(3)],
            from_north[5 + f],
            from_south[5 + f],
        )
    for f, ref in enumerate((spread, pulled, start.at[4])):
        to_mixed(ref, coef.at[f])
    one_step(
        [start.at[f] for f in range(4)],
        rows_at,
        [ahead.at[f] for f in range(4)],
        rows_at,
        coef_refs(coef),
        None,
    )
    take_patches(ahead, spread, pulled, start.at[2], cells, table, tmp, out)


def coef_refs(coef):
    return [coef.at[f] for f in range(3)]


def take_patches(after, spread, a_s, before_v, cells, table, tmp, out):
    refs = [after.at[2], after.at[0], after.at[3], spread, after.at[1], a_s, before_v]
    extract(refs, cells, table, tmp, out)


def port_places(ports):
    return [ports[k * 8 : k * 8 + 8, :].astype(jnp.int32) for k in range(3)]


def port_sim(got, codes, rows, cols, partner):
    got_t = [jnp.transpose(got[pl.ds(k, 128, stride=2), :]) for k in range(2)]
    fields = [{} for _ in range(7)]
    for index, (field, cell) in enumerate(patch_plan()):
        at = index * 8 % LANES
        fields[field][cell] = got_t[index * 8 // LANES][at : at + 8]
    v, s, u, spread, e, a_s, before = fields
    device = partner // 8
    slot = partner % 8

    def near(f, cell):
        a, b = cell
        left = jnp.where(cols == -b, f[cell], f[(a, b - 1)])
        right = jnp.where(cols == 4095 - b, f[cell], f[(a, b + 1)])
        return f[(a - 1, b)] + f[(a + 1, b)] + left + right

    def gain_of(here):
        theirs = jnp.zeros_like(here)
        for k in range(8):
            line = jnp.broadcast_to(here[k : k + 1], here.shape)
            theirs = jnp.where(slot == k, jnp.take_along_axis(line, device, axis=1), theirs)
        return 0.2 * (theirs - here)

    def add_gain(f, gain, reach):
        added = dict(f)
        index = 0
        for k in range(8):
            turned = pltpu.roll(gain, k, 0) if k else gain
            for shift in NEAR_LANES:
                moved = pltpu.roll(turned, (-shift) % LANES, 1) if shift else turned
                code = codes[index]
                index += 1
                for c in diamond(reach):
                    key = (c[0] * ROW_KEY + c[1]) & KEY_MASK
                    added[c] = added[c] + jnp.where(code == key, moved, 0.0)
        return added

    gains = [gain_of(before[(0, 0)])]
    v = add_gain(v, gains[0], RADIUS)
    for step in range(RADIUS + 1):
        gains.append(gain_of(v[(0, 0)]))
        reach = RADIUS - 1 - step
        if reach < 0:
            break
        parts = {c: reciprocals(s[c], e.get(c)) for c in diamond(reach)}
        new_v = {}
        for c in diamond(reach):
            new_v[c] = v_step(parts[c], v[c], u[c], near(v, c), spread[c])
        new_s, new_u = {}, {}
        for c in diamond(reach - 1):
            new_s[c] = s_step(parts[c], s[c], e[c], v[c], near(s, c), spread[c], a_s[c])
            new_u[c] = u_step(parts[c], v[c], u[c], near(u, c), spread[c])
        v = add_gain(new_v, gains[-1], reach)
        s, u = new_s, new_u
    return gains


def reciprocals(s, e):
    half, whole = s + 0.5, s + 1.0
    both = half * whole
    if e is None:
        inv = 1.0 / both
        return inv * whole, inv * half, None
    end = e + 1.0
    inv = 1.0 / (both * end)
    rest = inv * end
    return rest * whole, rest * half, inv * both


def s_step(parts, s, e, v, near, spread, a_s):
    return (
        a_s
        + s * (0.97 - 4.0 * spread)
        + 0.03 * e
        - 0.08
        + 0.04 * jnp.tanh(v + 0.3)
        + 0.06 * parts[0]
        + spread * near
    )


def e_step(s, e, near, spread, a_e):
    return a_e + e * (0.88 - 4.0 * spread) + 0.03 * s + spread * near


def v_step(parts, v, u, near, spread):
    return (
        v * (0.71 - 4.0 * spread + 0.15 * parts[1])
        + 0.18 * parts[1]
        - 0.23
        + 0.04 * u
        + spread * near
    )


def u_step(parts, v, u, near, spread):
    return (
        u * (0.78 - 4.0 * spread + 0.1 * parts[2])
        + 0.12 * parts[2]
        - 0.152
        + 0.04 * v
        + spread * near
    )


def make_codes(rows, cols, codes):
    key = rows * ROW_KEY + cols
    index = 0
    for k in range(8):
        turned = pltpu.roll(key, k, 0) if k else key
        for shift in NEAR_LANES:
            moved = pltpu.roll(turned, (-shift) % LANES, 1) if shift else turned
            codes[index] = (moved - key) & KEY_MASK
            index += 1


def my_column(value):
    lane_of = lax.axis_index("circ") * 16 + lax.axis_index("axial")
    tiles = []
    lane = iota((8, LANES), 1)
    for shift in NEAR_LANES:
        at = (lane_of + shift) & (LANES - 1)
        tiles.append(jnp.sum(jnp.where(lane == at, value, 0.0), axis=1, keepdims=True))
    tiles.append(jnp.zeros((NEAR_PORTS - 8 * len(tiles), 1), jnp.float32))
    return jnp.concatenate(tiles, axis=0)


def injections(gains, in_row, in_col, inject):
    pick = in_row[...].astype(jnp.bfloat16)
    zero = jnp.zeros((256 - 3 * NEAR_PORTS, WIDE), jnp.bfloat16)
    for k, gain in enumerate(gains):
        parts = three_parts(in_col[...] * my_column(gain))
        total = dot(pick, jnp.concatenate(list(parts) + [zero], axis=0))
        for tile in range(3):
            inject[k, tile] = total[:, tile * LANES : (tile + 1) * LANES]


def one_step(now, now_at, later, later_at, coef, inject):
    lane = iota((8, LANES), 1)
    i_axial = lax.axis_index("axial")
    head = lane == 0
    tail = lane == LANES - 1
    is_first = (lane * 0 + i_axial) == 0
    is_last = (lane * 0 + i_axial) == 15

    def load(f, tile, j):
        if j < 0:
            return pltpu.roll(now[f][tile, now_at(STEP - 1), :], 1, 0)
        if j == STEP:
            return pltpu.roll(now[f][tile, now_at(0), :], 7, 0)
        return now[f][tile, now_at(j), :]

    for j in range(STEP):
        mid, near = [], []
        for f in range(4):
            x = [load(f, tile, j) for tile in range(3)]
            left = [pltpu.roll(y, 1, 1) for y in x]
            right = [pltpu.roll(y, LANES - 1, 1) for y in x]
            lefts = [
                jnp.where(head, jnp.where(is_first, x[0], left[2]), left[0]),
                jnp.where(head, left[0], left[1]),
                jnp.where(head, left[1], left[2]),
            ]
            rights = [
                jnp.where(tail, right[1], right[0]),
                jnp.where(tail, jnp.where(is_last, x[1], right[2]), right[1]),
                jnp.where(tail, right[0], right[2]),
            ]
            mid.append(x)
            near.append(
                [
                    (load(f, tile, j - 1) + load(f, tile, j + 1)) + (lefts[tile] + rights[tile])
                    for tile in range(3)
                ]
            )
        for tile in range(3):
            s, e, v, u = [x[tile] for x in mid]
            n = [x[tile] for x in near]
            spread = coef[0][tile, mixed_at(j), :]
            parts = reciprocals(s, e)
            new_s = s_step(parts, s, e, v, n[0], spread, coef[1][tile, mixed_at(j), :])
            new_e = e_step(s, e, n[1], spread, coef[2][tile, mixed_at(j), :])
            new_v = v_step(parts, v, u, n[2], spread)
            if inject is not None:
                new_v = new_v + inject[tile, mixed_at(j), :]
            later[0][tile, later_at(j), :] = new_s
            later[1][tile, later_at(j), :] = new_e
            later[2][tile, later_at(j), :] = new_v
            later[3][tile, later_at(j), :] = u_step(parts, v, u, n[3], spread)


def coupled_steps(ahead, coef, got, ports, in_row, in_col, codes, state, inject):
    rows, cols, partner = port_places(ports)
    gains = port_sim(got, codes, rows, cols, partner)
    injections(gains, in_row, in_col, inject)
    for f in range(4):
        to_mixed(ahead.at[f], state.at[0, f])
    state[0, 2] = state[0, 2] + inject[0]

    def one(k, carry):
        now = lax.rem(k, 2)
        one_step(
            [state.at[now, f] for f in range(4)],
            mixed_at,
            [state.at[1 - now, f] for f in range(4)],
            mixed_at,
            coef,
            inject.at[k + 1],
        )
        return carry

    lax.fori_loop(0, 3, one, 0)


def first_steps_kernel(
    cells, ahead, spread, pulled, coef, got, ports, in_row, in_col, codes, table,
    later, out, state, inject, tmp,
):
    coefs = coef_refs(coef)
    coupled_steps(ahead, coefs, got, ports, in_row, in_col, codes, state, inject)
    for tile in range(3):
        for j in range(STEP):
            later[4, tile, rows_at(j), :] = state[1, 2, tile, mixed_at(j), :]
    one_step(
        [state.at[1, f] for f in range(4)],
        mixed_at,
        [later.at[f] for f in range(4)],
        rows_at,
        coefs,
        None,
    )
    take_patches(later, spread, pulled, later.at[4], cells, table, tmp, out)


def last_steps_kernel(
    ahead, coef, got, ports, in_row, in_col, codes, ca_out, vo_out, state, inject
):
    coefs = coef_refs(coef)
    coupled_steps(ahead, coefs, got, ports, in_row, in_col, codes, state, inject)
    for f in range(4):
        out = (ca_out, vo_out)[f // 2].at[f % 2]
        for tile in range(2):
            for j in range(STEP):
                state[0, f, tile, rows_at(j), :] = state[1, f, tile, mixed_at(j), :]
            out[:, tile * LANES : (tile + 1) * LANES] = state[0, f, tile, HALO : HALO + 128, :]


def shifted(value, axis, step, periodic):
    count = lax.axis_size(axis)
    pairs = [(i, i + step) for i in range(count)]
    if periodic:
        pairs = [(i, j % count) for i, j in pairs]
    return lax.ppermute(value, axis, [(i, j) for i, j in pairs if 0 <= j < count])


def swap_axial(to_west, to_east):
    return shifted(to_west, "axial", -1, False), shifted(to_east, "axial", 1, False)


def swap_circ(to_north, to_south):
    return shifted(to_south, "circ", 1, True), shifted(to_north, "circ", -1, True)


def to_all(value):
    blocks = value.reshape(128, 1, -1)
    return lax.all_to_all(blocks, AXES, 0, 0, tiled=True).reshape(value.shape)


def local(ca, vo, co, fluid, target, row, count, cells, partner):
    table = jnp.asarray(patch_table())
    field = (3, EXT, LANES)
    lines = fluid.reshape(-1, 2, 2, LANES).transpose(0, 2, 1, 3).reshape(-1, LANES)
    (packed,) = call(pack_kernel, [(128 * BLOCK, LANES)], [SMEM] * 3 + [VMEM] * 3, "pack", room=60)(
        count, cells, partner, target.reshape(1, -1), row.reshape(1, -1), lines
    )
    received = to_all(packed)
    to_west, to_east = call(strips_kernel, [(5 * HALO, LANES)] * 2, [HELD] * 3, "strips")(
        ca, vo, co
    )
    from_east, from_west = swap_axial(to_west, to_east)
    (sides,) = call(sides_kernel, [(5, 128, LANES)], [HELD] * 2, "sides")(from_east, from_west)
    ring = (7, 3, HALO, LANES)
    force, ports, to_north, to_south = call(
        force_kernel, [(2, 3, 128, LANES), (24, LANES), ring, ring], [HELD] * 5, "force"
    )(received, ca, vo, co, sides)
    from_north, from_south = swap_circ(to_north, to_south)
    in_row, in_col, codes = call(
        tables_kernel,
        [(EXT, 256), (NEAR_PORTS, WIDE), (72, 8, LANES)],
        [HELD],
        "tables",
        last=jnp.int32,
    )(ports)
    patch_space = pltpu.VMEM((64, LANES), jnp.float32)
    ahead, coef, spread, pulled, patches = call(
        first_patch_kernel,
        [(4, *field), (3, *field), field, field, (256, LANES)],
        [SMEM] + [HELD] * 8,
        "first_patch",
        [pltpu.VMEM((5, *field), jnp.float32), patch_space],
    )(cells, ca, vo, co, sides, from_north, from_south, force, table)
    got = to_all(patches)
    scratch = [pltpu.VMEM((2, 4, *field), jnp.float32), pltpu.VMEM((4, *field), jnp.float32)]
    ahead, patches = call(
        first_steps_kernel,
        [(5, *field), (256, LANES)],
        [SMEM] + [HELD] * 10,
        "first_steps",
        scratch + [patch_space],
    )(cells, ahead, spread, pulled, coef, got, ports, in_row, in_col, codes, table)
    got = to_all(patches)
    return call(
        last_steps_kernel,
        [(2, 128, 256)] * 2,
        [HELD] * 7,
        "last_steps",
        scratch,
        place=jax.ShapeDtypeStruct,
    )(ahead, coef, got, ports, in_row, in_col, codes)


def solution(mesh):
    return jax.shard_map(
        local,
        mesh=mesh,
        in_specs=(
            P(None, "circ", "axial"),
            P(None, "circ", "axial"),
            P("circ", "axial"),
            P(AXES, None, None),
            P(AXES, None),
            P(AXES),
            P(AXES),
            P(AXES),
            P(AXES),
        ),
        out_specs=(P(None, "circ", "axial"), P(None, "circ", "axial")),
        check_vma=False,
    )
```

```python
import functools

import jax
import jax.numpy as jnp
import numpy as np
from jax import lax
from jax.experimental import pallas as pl
from jax.experimental.pallas import tpu as pltpu
from jax.sharding import PartitionSpec as P

AXES = ("circ", "axial")
HALO = 8
LANES = 128
WIDE = 384
RADIUS = 2
SIDE = 5
BLOCK = 9
EXT = 144
STEP = 18
NEAR_PORTS = 80
NEAR_LANES = (0, 1, -1, 16, -16, 15, -15, 17, -17)
ROW_KEY = 8192
KEY_MASK = 1024 * ROW_KEY - 1
VMEM = pl.BlockSpec(memory_space=pltpu.VMEM)
SMEM = pl.BlockSpec(memory_space=pltpu.SMEM)


def diamond(radius):
    if radius < 0:
        return []
    span = range(-radius, radius + 1)
    return [(a, b) for a in span for b in span if abs(a) + abs(b) <= radius]


def reachable(shift, radius):
    down = {-17: -1, -16: -1, -15: -1, 15: 1, 16: 1, 17: 1}.get(shift, 0)
    right = {-17: -1, -1: -1, 15: -1, -15: 1, 1: 1, 17: 1}.get(shift, 0)
    return [(a, b) for a, b in diamond(radius) if a * down >= abs(down) and b * right >= abs(right)]


def patch_plan():
    radii = (2, 1, 1, 1, 0, 0, 0)
    return [(field, cell) for field, r in enumerate(radii) for cell in diamond(r)]


def patch_table():
    table = np.full((8, 2 * LANES), -1, np.int32)
    for index, (field, (a, b)) in enumerate(patch_plan()):
        for slot in range(8):
            at = index * 8 + slot
            table[0, at] = field * SIDE + b + RADIUS
            table[1, at] = slot * 8 + a + RADIUS
    return table


def iota(shape, dim):
    return lax.broadcasted_iota(jnp.int32, shape, dim)


HELD = pl.BlockSpec(memory_space=pltpu.VMEM)


def call(kernel, outs, ins, name, scratch=(), last=jnp.float32, place=pltpu.VMEM, room=20):
    types = [jnp.float32] * (len(outs) - 1) + [last]
    run = pl.pallas_call(
        kernel,
        out_shape=tuple(place(s, t) for s, t in zip(outs, types)),
        in_specs=ins,
        out_specs=tuple(VMEM for _ in outs),
        scratch_shapes=list(scratch),
        name=name,
        compiler_params=pltpu.CompilerParams(vmem_limit_bytes=room * 1024 * 1024),
    )

    def placed(*args):
        return run(
            *(
                pltpu.with_memory_space_constraint(x, pltpu.VMEM) if spec is HELD else x
                for x, spec in zip(args, ins)
            )
        )

    return placed


def side_strips(tiles):
    rows = tiles[0][0].shape[0]
    lane = iota((rows, LANES), 1)
    left = jnp.zeros((rows, LANES), jnp.float32)
    right = left
    for f, (first, last) in enumerate(tiles):
        mine = (lane >= f * HALO) & (lane < (f + 1) * HALO)
        left = jnp.where(mine, pltpu.roll(first, f * HALO, 1) if f else first, left)
        right = jnp.where(mine, pltpu.roll(last, f * HALO + HALO, 1), right)
    return left, right


def side_tile(from_east, from_west, f):
    lane = iota(from_east.shape, 1)
    east = pltpu.roll(from_east, (LANES - f * HALO) % LANES, 1) if f else from_east
    west = pltpu.roll(from_west, LANES - HALO - f * HALO, 1)
    return jnp.where(lane < HALO, east, jnp.where(lane >= LANES - HALO, west, 0.0))


def three_parts(x):
    high = x.astype(jnp.bfloat16)
    rest = x - high.astype(jnp.float32)
    middle = rest.astype(jnp.bfloat16)
    low = (rest - middle.astype(jnp.float32)).astype(jnp.bfloat16)
    return high, middle, low


def one_hot(pick):
    return jnp.where(pick, 1.0, 0.0).astype(jnp.bfloat16)


def dot(a, b):
    return jnp.dot(a, b, preferred_element_type=jnp.float32)


def exact_pick(pick, x):
    pick = one_hot(pick)
    high, middle, low = three_parts(x)
    return dot(pick, low) + dot(pick, middle) + dot(pick, high)


def all_fields(ca, vo, co):
    return [ca.at[0], ca.at[1], vo.at[0], vo.at[1], co]


def strips_kernel(ca, vo, co, to_west, to_east):
    left, right = side_strips([(f[:, :LANES], f[:, LANES:]) for f in all_fields(ca, vo, co)])
    to_west[...] = jnp.transpose(left)[: 5 * HALO]
    to_east[...] = jnp.transpose(right)[: 5 * HALO]


def sides_kernel(from_east, from_west, sides):
    blank = jnp.zeros((LANES - 5 * HALO, LANES), jnp.float32)
    east = jnp.transpose(jnp.concatenate([from_east[...], blank], axis=0))
    west = jnp.transpose(jnp.concatenate([from_west[...], blank], axis=0))
    for f in range(5):
        sides[f] = side_tile(east, west, f)


def lanes_to(x, source, target, count):
    lane = iota(x.shape, 1)
    turned = pltpu.roll(x, (target - source) % LANES, 1) if target != source else x
    return jnp.where((lane >= target) & (lane < target + count), turned, 0.0)


def pack_kernel(count, cells, partner, target, row, fluid, packed):
    i_circ = lax.axis_index("circ")
    i_axial = lax.axis_index("axial")
    slots = fluid.shape[0] // 4
    t_row = target[...]
    order = iota((1, slots), 1)
    used = order < count[0]
    eye = iota((slots, slots), 0) == iota((slots, slots), 1)
    t_col = jnp.sum(jnp.where(eye, t_row, 0), axis=1, keepdims=True)
    earlier = (
        (t_col == t_row)
        & (iota((slots, slots), 0) < count[0])
        & (iota((slots, slots), 0) < iota((slots, slots), 1))
    )
    rank = jnp.sum(jnp.where(earlier, 1, 0), axis=0, keepdims=True)
    place = jnp.where(used, rank * 128 + t_row, -1)
    pick = iota((256, slots), 0) == place
    tags = jnp.sum(jnp.where(pick, row[...] + 1, 0), axis=1, keepdims=True).astype(jnp.float32)
    tags0, tags1 = tags[:128], tags[128:]
    tiles = [fluid[pl.ds(c * 2 + k, slots, stride=4), :] for k in range(2) for c in range(2)]
    moved = exact_pick(pick, jnp.concatenate(tiles, axis=1))
    for half in range(2):
        for part in range(4):
            packed[pl.ds(half * 4 + part, 128, stride=BLOCK), :] = moved[
                half * 128 : half * 128 + 128, part * LANES : part * LANES + LANES
            ]
    lane = iota((128, LANES), 1)
    tail = jnp.where(lane == 0, tags0, jnp.where(lane == 1, tags1, 0.0))
    for slot in range(8):
        cell = cells[slot]
        for base, value in (
            (8, i_circ * 128 + cell // 256),
            (16, i_axial * 256 + cell % 256),
            (24, partner[slot]),
        ):
            tail = jnp.where(lane == base + slot, value.astype(jnp.float32), tail)
    east = jnp.where(lane == 2, tags0, jnp.where(lane == 3, tags1, 0.0))
    west = jnp.where(lane == 4, tags0, jnp.where(lane == 5, tags1, 0.0))
    for half in range(2):
        rows = moved[half * 128 : half * 128 + 128]
        for k in range(2):
            first = rows[:, 2 * k * LANES : (2 * k + 1) * LANES]
            last = rows[:, (2 * k + 1) * LANES : (2 * k + 2) * LANES]
            east = east + lanes_to(first, 0, 32 + half * 16 + k * HALO, HALO)
            west = west + lanes_to(last, LANES - HALO, 64 + half * 16 + k * HALO, HALO)
    tail = tail + pltpu.roll(east, 127, 0) + pltpu.roll(west, 1, 0)
    packed[pl.ds(8, 128, stride=BLOCK), :] = tail


def force_kernel(got, ca, vo, co, sides, force, ports, to_north, to_south):
    tail = got[pl.ds(8, 128, stride=BLOCK), :]
    tail_t = jnp.transpose(tail)
    ports[...] = tail_t[8:32]
    line = iota((128, 128), 0).astype(jnp.float32) + 1.0

    def pair(k):
        return jnp.concatenate([tail_t[k : k + 1] == line, tail_t[k + 1 : k + 2] == line], axis=1)

    blocks = [
        jnp.concatenate(
            [got[pl.ds(half * 4 + part, 128, stride=BLOCK), :] for half in range(2)], axis=0
        )
        for part in range(4)
    ]
    total = exact_pick(pair(0), jnp.concatenate(blocks, axis=1))
    both = jnp.concatenate([tail, pltpu.roll(tail, LANES - 16, 1)], axis=0)
    both = jnp.concatenate(three_parts(both), axis=1)
    east, west = dot(one_hot(pair(2)), both), dot(one_hot(pair(4)), both)
    east, west = [x[:, 256:] + x[:, 128:256] + x[:, :128] for x in (east, west)]
    for tile in range(3):
        if tile < 2:
            shear = total[:, tile * LANES : (tile + 1) * LANES]
            agonist = total[:, (tile + 2) * LANES : (tile + 3) * LANES]
        else:
            shear, agonist = [
                lanes_to(east, 32 + k * HALO, 0, HALO)
                + lanes_to(west, 64 + k * HALO, LANES - HALO, HALO)
                for k in range(2)
            ]
        stress = shear * shear / (1.0 + shear * shear)
        stimulus = 0.5 + 0.5 * jnp.tanh(0.5 * agonist)
        a_s = 0.1 * stimulus
        a_e = 0.02 + 0.15 * stress + 0.04 * stimulus
        for f, value in enumerate((a_s, a_e)):
            force[f, tile] = value
            to_north[5 + f, tile] = value[:HALO]
            to_south[5 + f, tile] = value[128 - HALO :]
    for f, ref in enumerate(all_fields(ca, vo, co)):
        for rows, out in ((slice(0, HALO), to_north), (slice(128 - HALO, 128), to_south)):
            out[f, 0] = ref[rows, :LANES]
            out[f, 1] = ref[rows, LANES:]
            out[f, 2] = sides[f, rows, :]


def extract(fields, cells, table, tmp, out):
    lane = iota((8, LANES), 1)
    long_lane = iota((16, LANES), 1)
    for slot in range(8):
        cell = cells[slot]
        row = cell // 256 + HALO - RADIUS
        col = lax.rem(cell % 256 - RADIUS + WIDE, WIDE)
        base = pl.multiple_of(row // 8 * 8, 8)
        turn = 16 - (row - base)
        tile = col // LANES
        other = lax.rem(tile + 1, 3)
        inside = col % LANES
        kept = jnp.zeros((8, LANES), jnp.float32)
        for f, field in enumerate((2, 0, 3, 5, 1, 6, 4)):
            window = jnp.where(
                long_lane < inside,
                fields[other, field, pl.ds(base, 16), :],
                fields[tile, field, pl.ds(base, 16), :],
            )
            window = pltpu.roll(window, turn, 0)[:8]
            window = pltpu.roll(window, (2 * LANES - inside + f * SIDE) % LANES, 1)
            kept = jnp.where((lane >= f * SIDE) & (lane < (f + 1) * SIDE), window, kept)
        tmp[slot * 8 : slot * 8 + 8, :] = kept
    width = 2 * LANES
    at = iota((LANES, width), 0)
    wanted = table[0:1, :]
    pick = one_hot((at == wanted) | (at == wanted + 40) | (at == wanted + 80))
    high, middle, low = [x.astype(jnp.float32) for x in three_parts(tmp[...])]
    pieces = dot(
        (high + pltpu.roll(middle, 40, 1) + pltpu.roll(low, 80, 1)).astype(jnp.bfloat16), pick
    )
    mine = iota((64, width), 0) == table[1:2, :]
    line = jnp.sum(jnp.where(mine, pieces, 0.0), axis=0, keepdims=True)
    for k in range(2):
        out[pl.ds(k, 128, stride=2), :] = jnp.broadcast_to(
            line[:, k * LANES : (k + 1) * LANES], (128, LANES)
        )


class Field:
    def __init__(self, ref, f):
        self.ref, self.f = ref, f

    def __getitem__(self, at):
        return self.ref[(at[0], self.f) + at[1:]]

    def __setitem__(self, at, value):
        self.ref[(at[0], self.f) + at[1:]] = value


def fields_of(ref, count):
    return [Field(ref, f) for f in range(count)]


def build_rows(dst, tiles, north, south):
    for tile in range(3):
        dst[tile, slice(HALO, HALO + 128), :] = tiles[tile]
        dst[tile, slice(0, HALO), :] = north[tile]
        dst[tile, slice(HALO + 128, EXT), :] = south[tile]


def rows_at(j):
    return pl.ds(j, 8, stride=STEP)


def mixed_at(j):
    return pl.ds(8 * j, 8)


def to_mixed(src, dst):
    for tile in range(3):
        for j in range(STEP):
            dst[tile, mixed_at(j), :] = src[tile, rows_at(j), :]


def tables_kernel(ports, in_row, in_col, codes):
    rows, cols, _ = port_places(ports)
    make_codes(rows, cols, codes)
    i_circ = lax.axis_index("circ")
    i_axial = lax.axis_index("axial")
    row = my_column(rows.astype(jnp.float32)).astype(jnp.int32)
    col = my_column(cols.astype(jnp.float32)).astype(jnp.int32)
    row = (row - i_circ * 128 + HALO) & 1023
    col = col - i_axial * 256
    ok = (iota((NEAR_PORTS, 1), 0) < 72) & (col >= -HALO) & (col < 256 + HALO) & (row < EXT)
    col = jnp.where(ok, jnp.where(col < 0, col + WIDE, col), -1)
    group = lax.shift_right_logical(row * 57, 10)
    place = jnp.where(ok, (row - group * STEP) * 8 + group, -1)
    in_col[...] = jnp.where(col == iota((NEAR_PORTS, WIDE), 1), 1.0, 0.0)
    place = jnp.concatenate([place, place, place, jnp.full((16, 1), -1, jnp.int32)], axis=0)
    in_row[...] = jnp.transpose(jnp.where(place == iota((256, 256), 1), 1.0, 0.0))[:EXT]


def first_patch_kernel(
    cells, ca, vo, co, sides, from_north, from_south, force, table,
    ahead, coef, out, start, tmp,
):
    after = fields_of(ahead, 7)
    before = fields_of(start, 5)
    for f, ref in enumerate(all_fields(ca, vo, co)):
        scale = 0.05 if f == 4 else 1.0
        build_rows(
            before[f] if f < 4 else after[5],
            [t * scale for t in (ref[:, :LANES], ref[:, LANES:], sides[f])],
            from_north[f] * scale,
            from_south[f] * scale,
        )
    for f in range(2):
        build_rows(
            after[6] if f == 0 else before[4],
            [force[f, tile] for tile in range(3)],
            from_north[5 + f],
            from_south[5 + f],
        )
    for tile in range(3):
        ahead[tile, 4] = start[tile, 2]
    coefs = fields_of(coef, 3)
    for src, dst in zip((after[5], after[6], before[4]), coefs):
        to_mixed(src, dst)
    one_step(before[:4], rows_at, after[:4], rows_at, coefs, None)
    extract(ahead, cells, table, tmp, out)


def port_places(ports):
    return [ports[k * 8 : k * 8 + 8, :].astype(jnp.int32) for k in range(3)]


def port_sim(got, codes, rows, cols, partner):
    got_t = [jnp.transpose(got[pl.ds(k, 128, stride=2), :]) for k in range(2)]
    fields = [{} for _ in range(7)]
    for index, (field, cell) in enumerate(patch_plan()):
        at = index * 8 % LANES
        fields[field][cell] = got_t[index * 8 // LANES][at : at + 8]
    v, s, u, spread, e, a_s, before = fields
    device = partner // 8
    slot = partner % 8

    def near(f, cell):
        a, b = cell
        left = jnp.where(cols == -b, f[cell], f[(a, b - 1)])
        right = jnp.where(cols == 4095 - b, f[cell], f[(a, b + 1)])
        return f[(a - 1, b)] + f[(a + 1, b)] + left + right

    def gain_of(here):
        theirs = jnp.zeros_like(here)
        for k in range(8):
            line = jnp.broadcast_to(here[k : k + 1], here.shape)
            theirs = jnp.where(slot == k, jnp.take_along_axis(line, device, axis=1), theirs)
        return 0.2 * (theirs - here)

    def add_gain(f, gain, reach):
        added = dict(f)
        for k in range(8):
            turned = pltpu.roll(gain, k, 0) if k else gain
            for place, shift in enumerate(NEAR_LANES):
                cells = reachable(shift, reach)
                if not cells:
                    continue
                moved = pltpu.roll(turned, (-shift) % LANES, 1) if shift else turned
                code = codes[k * len(NEAR_LANES) + place]
                for c in cells:
                    key = (c[0] * ROW_KEY + c[1]) & KEY_MASK
                    added[c] = added[c] + jnp.where(code == key, moved, 0.0)
        return added

    gains = [gain_of(before[(0, 0)])]
    v = add_gain(v, gains[0], RADIUS)
    for step in range(RADIUS + 1):
        gains.append(gain_of(v[(0, 0)]))
        reach = RADIUS - 1 - step
        if reach < 0:
            break
        parts = {c: reciprocals(s[c], e.get(c)) for c in diamond(reach)}
        new_v = {}
        for c in diamond(reach):
            new_v[c] = v_step(parts[c], v[c], u[c], near(v, c), spread[c])
        new_s, new_u = {}, {}
        for c in diamond(reach - 1):
            new_s[c] = s_step(parts[c], s[c], e[c], v[c], near(s, c), spread[c], a_s[c])
            new_u[c] = u_step(parts[c], v[c], u[c], near(u, c), spread[c])
        v = add_gain(new_v, gains[-1], reach)
        s, u = new_s, new_u
    return gains


def reciprocals(s, e):
    half, whole = s + 0.5, s + 1.0
    both = half * whole
    if e is None:
        inv = 1.0 / both
        return inv * whole, inv * half, None
    end = e + 1.0
    inv = 1.0 / (both * end)
    rest = inv * end
    return rest * whole, rest * half, inv * both


def s_step(parts, s, e, v, near, spread, a_s):
    return (
        a_s
        + s * (0.97 - 4.0 * spread)
        + 0.03 * e
        - 0.08
        + 0.04 * jnp.tanh(v + 0.3)
        + 0.06 * parts[0]
        + spread * near
    )


def e_step(s, e, near, spread, a_e):
    return a_e + e * (0.88 - 4.0 * spread) + 0.03 * s + spread * near


def v_step(parts, v, u, near, spread):
    return (
        v * (0.71 - 4.0 * spread + 0.15 * parts[1])
        + 0.18 * parts[1]
        - 0.23
        + 0.04 * u
        + spread * near
    )


def u_step(parts, v, u, near, spread):
    return (
        u * (0.78 - 4.0 * spread + 0.1 * parts[2])
        + 0.12 * parts[2]
        - 0.152
        + 0.04 * v
        + spread * near
    )


def make_codes(rows, cols, codes):
    key = rows * ROW_KEY + cols
    index = 0
    for k in range(8):
        turned = pltpu.roll(key, k, 0) if k else key
        for shift in NEAR_LANES:
            moved = pltpu.roll(turned, (-shift) % LANES, 1) if shift else turned
            codes[index] = (moved - key) & KEY_MASK
            index += 1


def my_column(value):
    lane_of = lax.axis_index("circ") * 16 + lax.axis_index("axial")
    tiles = []
    lane = iota((8, LANES), 1)
    for shift in NEAR_LANES:
        at = (lane_of + shift) & (LANES - 1)
        tiles.append(jnp.sum(jnp.where(lane == at, value, 0.0), axis=1, keepdims=True))
    tiles.append(jnp.zeros((NEAR_PORTS - 8 * len(tiles), 1), jnp.float32))
    return jnp.concatenate(tiles, axis=0)


def injections(gains, in_row, in_col, inject):
    pick = in_row[...].astype(jnp.bfloat16)
    lane_of = lax.axis_index("circ") * 16 + lax.axis_index("axial")
    zero = jnp.zeros((NEAR_PORTS - 8 * len(NEAR_LANES), WIDE), jnp.float32)
    blank = jnp.zeros((256 - 3 * NEAR_PORTS, WIDE), jnp.bfloat16)
    for k, gain in enumerate(gains):
        lines = []
        for place, shift in enumerate(NEAR_LANES):
            at = jnp.zeros((8, LANES), jnp.int32) + ((lane_of + shift) & (LANES - 1))
            mine = jnp.take_along_axis(gain, at, axis=1)
            rows = slice(place * 8, place * 8 + 8)
            lines.append(in_col[rows, :] * jnp.concatenate([mine] * 3, axis=1))
        parts = three_parts(jnp.concatenate(lines + [zero], axis=0))
        total = dot(pick, jnp.concatenate(list(parts) + [blank], axis=0))
        for tile in range(3):
            inject[k, tile] = total[:, tile * LANES : (tile + 1) * LANES]


def one_step(now, now_at, later, later_at, coef, inject):
    lane = iota((8, LANES), 1)
    i_axial = lax.axis_index("axial")
    head = lane == 0
    tail = lane == LANES - 1
    is_first = (lane * 0 + i_axial) == 0
    is_last = (lane * 0 + i_axial) == 15

    def load(f, tile, j):
        if j < 0:
            return pltpu.roll(now[f][tile, now_at(STEP - 1), :], 1, 0)
        if j == STEP:
            return pltpu.roll(now[f][tile, now_at(0), :], 7, 0)
        return now[f][tile, now_at(j), :]

    for j in range(STEP):
        mid, near = [], []
        for f in range(4):
            x = [load(f, tile, j) for tile in range(3)]
            left = [pltpu.roll(y, 1, 1) for y in x]
            right = [pltpu.roll(y, LANES - 1, 1) for y in x]
            lefts = [
                jnp.where(head, jnp.where(is_first, x[0], left[2]), left[0]),
                jnp.where(head, left[0], left[1]),
                jnp.where(head, left[1], left[2]),
            ]
            rights = [
                jnp.where(tail, right[1], right[0]),
                jnp.where(tail, jnp.where(is_last, x[1], right[2]), right[1]),
                jnp.where(tail, right[0], right[2]),
            ]
            mid.append(x)
            near.append(
                [
                    (load(f, tile, j - 1) + load(f, tile, j + 1)) + (lefts[tile] + rights[tile])
                    for tile in range(3)
                ]
            )
        for tile in range(3):
            s, e, v, u = [x[tile] for x in mid]
            n = [x[tile] for x in near]
            spread = coef[0][tile, mixed_at(j), :]
            parts = reciprocals(s, e)
            new_s = s_step(parts, s, e, v, n[0], spread, coef[1][tile, mixed_at(j), :])
            new_e = e_step(s, e, n[1], spread, coef[2][tile, mixed_at(j), :])
            new_v = v_step(parts, v, u, n[2], spread)
            if inject is not None:
                new_v = new_v + inject[tile, mixed_at(j), :]
            later[0][tile, later_at(j), :] = new_s
            later[1][tile, later_at(j), :] = new_e
            later[2][tile, later_at(j), :] = new_v
            later[3][tile, later_at(j), :] = u_step(parts, v, u, n[3], spread)


def coupled_steps(ahead, coef, got, ports, in_row, in_col, codes, first, second, inject):
    rows, cols, partner = port_places(ports)
    gains = port_sim(got, codes, rows, cols, partner)
    injections(gains, in_row, in_col, inject)
    one, two = fields_of(first, 4), fields_of(second, 4)
    for f in range(4):
        for tile in range(3):
            for j in range(STEP):
                value = ahead[tile, f, rows_at(j), :]
                if f == 2:
                    value = value + inject[0, tile, mixed_at(j), :]
                first[tile, f, mixed_at(j), :] = value
    coefs = fields_of(coef, 3)
    for k, (now, later) in enumerate(((one, two), (two, one), (one, two))):
        one_step(now, mixed_at, later, mixed_at, coefs, inject.at[k + 1])
    return two


def first_steps_kernel(
    cells, ahead, coef, got, ports, in_row, in_col, codes, table,
    later, out, first, second, inject, tmp,
):
    now = coupled_steps(ahead, coef, got, ports, in_row, in_col, codes, first, second, inject)
    for tile in range(3):
        for j in range(STEP):
            later[tile, 4, rows_at(j), :] = second[tile, 2, mixed_at(j), :]
        later[tile, 5] = ahead[tile, 5]
        later[tile, 6] = ahead[tile, 6]
    one_step(now, mixed_at, fields_of(later, 4), rows_at, fields_of(coef, 3), None)
    extract(later, cells, table, tmp, out)


def last_steps_kernel(
    ahead, coef, got, ports, in_row, in_col, codes, ca_out, vo_out, first, second, inject
):
    coupled_steps(ahead, coef, got, ports, in_row, in_col, codes, first, second, inject)
    for f in range(4):
        out = (ca_out, vo_out)[f // 2].at[f % 2]
        for tile in range(2):
            for j in range(STEP):
                first[tile, f, rows_at(j), :] = second[tile, f, mixed_at(j), :]
            out[:, tile * LANES : (tile + 1) * LANES] = first[tile, f, HALO : HALO + 128, :]


def shifted(value, axis, step, periodic):
    count = lax.axis_size(axis)
    pairs = [(i, i + step) for i in range(count)]
    if periodic:
        pairs = [(i, j % count) for i, j in pairs]
    return lax.ppermute(value, axis, [(i, j) for i, j in pairs if 0 <= j < count])


def swap_axial(to_west, to_east):
    return shifted(to_west, "axial", -1, False), shifted(to_east, "axial", 1, False)


def swap_circ(to_north, to_south):
    return shifted(to_south, "circ", 1, True), shifted(to_north, "circ", -1, True)


def stack(count):
    return (3, count, EXT, LANES)


def to_all(value):
    blocks = value.reshape(128, 1, -1)
    return lax.all_to_all(blocks, AXES, 0, 0, tiled=True).reshape(value.shape)


def local(ca, vo, co, fluid, target, row, count, cells, partner):
    table = jnp.asarray(patch_table())
    lines = fluid.reshape(-1, 2, 2, LANES).transpose(0, 2, 1, 3).reshape(-1, LANES)
    (packed,) = call(pack_kernel, [(128 * BLOCK, LANES)], [SMEM] * 3 + [VMEM] * 3, "pack", room=60)(
        count, cells, partner, target.reshape(1, -1), row.reshape(1, -1), lines
    )
    received = to_all(packed)
    to_west, to_east = call(strips_kernel, [(5 * HALO, LANES)] * 2, [HELD] * 3, "strips")(
        ca, vo, co
    )
    from_east, from_west = swap_axial(to_west, to_east)
    (sides,) = call(sides_kernel, [(5, 128, LANES)], [HELD] * 2, "sides")(from_east, from_west)
    ring = (7, 3, HALO, LANES)
    force, ports, to_north, to_south = call(
        force_kernel, [(2, 3, 128, LANES), (24, LANES), ring, ring], [HELD] * 5, "force"
    )(received, ca, vo, co, sides)
    from_north, from_south = swap_circ(to_north, to_south)
    in_row, in_col, codes = call(
        tables_kernel,
        [(EXT, 256), (NEAR_PORTS, WIDE), (72, 8, LANES)],
        [HELD],
        "tables",
        last=jnp.int32,
    )(ports)
    patch_space = pltpu.VMEM((64, LANES), jnp.float32)
    ahead, coef, patches = call(
        first_patch_kernel,
        [stack(7), stack(3), (256, LANES)],
        [SMEM] + [HELD] * 8,
        "first_patch",
        [pltpu.VMEM(stack(5), jnp.float32), patch_space],
    )(cells, ca, vo, co, sides, from_north, from_south, force, table)
    got = to_all(patches)
    scratch = [pltpu.VMEM(stack(4), jnp.float32)] * 2 + [pltpu.VMEM((4, 3, EXT, LANES), jnp.float32)]
    ahead, patches = call(
        first_steps_kernel,
        [stack(7), (256, LANES)],
        [SMEM] + [HELD] * 8,
        "first_steps",
        scratch + [patch_space],
    )(cells, ahead, coef, got, ports, in_row, in_col, codes, table)
    got = to_all(patches)
    return call(
        last_steps_kernel,
        [(2, 128, 256)] * 2,
        [HELD] * 7,
        "last_steps",
        scratch,
        place=jax.ShapeDtypeStruct,
    )(ahead, coef, got, ports, in_row, in_col, codes)


def solution(mesh):
    return jax.shard_map(
        local,
        mesh=mesh,
        in_specs=(
            P(None, "circ", "axial"),
            P(None, "circ", "axial"),
            P("circ", "axial"),
            P(AXES, None, None),
            P(AXES, None),
            P(AXES),
            P(AXES),
            P(AXES),
            P(AXES),
        ),
        out_specs=(P(None, "circ", "axial"), P(None, "circ", "axial")),
        check_vma=False,
    )
```

```python
import functools

import jax
import jax.numpy as jnp
import numpy as np
from jax import lax
from jax.experimental import pallas as pl
from jax.experimental.pallas import tpu as pltpu
from jax.sharding import PartitionSpec as P

AXES = ("circ", "axial")
HALO = 8
LANES = 128
WIDE = 384
RADIUS = 2
SIDE = 5
BLOCK = 9
EXT = 144
STEP = 18
NEAR_PORTS = 80
NEAR_LANES = (0, 1, -1, 16, -16, 15, -15, 17, -17)
ROW_KEY = 8192
KEY_MASK = 1024 * ROW_KEY - 1
VMEM = pl.BlockSpec(memory_space=pltpu.VMEM)
SMEM = pl.BlockSpec(memory_space=pltpu.SMEM)


def diamond(radius):
    if radius < 0:
        return []
    span = range(-radius, radius + 1)
    return [(a, b) for a in span for b in span if abs(a) + abs(b) <= radius]


def reachable(shift, radius):
    down = {-17: -1, -16: -1, -15: -1, 15: 1, 16: 1, 17: 1}.get(shift, 0)
    right = {-17: -1, -1: -1, 15: -1, -15: 1, 1: 1, 17: 1}.get(shift, 0)
    return [(a, b) for a, b in diamond(radius) if a * down >= abs(down) and b * right >= abs(right)]


def patch_plan():
    radii = (2, 1, 1, 1, 0, 0, 0)
    return [(field, cell) for field, r in enumerate(radii) for cell in diamond(r)]


def patch_table():
    table = np.full((8, 2 * LANES), -1, np.int32)
    for index, (field, (a, b)) in enumerate(patch_plan()):
        for slot in range(8):
            at = index * 8 + slot
            table[0, at] = field * SIDE + b + RADIUS
            table[1, at] = slot * 8 + a + RADIUS
    return table


def iota(shape, dim):
    return lax.broadcasted_iota(jnp.int32, shape, dim)


HELD = pl.BlockSpec(memory_space=pltpu.VMEM)


def call(kernel, outs, ins, name, scratch=(), last=jnp.float32, place=pltpu.VMEM, room=20):
    types = [jnp.float32] * (len(outs) - 1) + [last]
    run = pl.pallas_call(
        kernel,
        out_shape=tuple(place(s, t) for s, t in zip(outs, types)),
        in_specs=ins,
        out_specs=tuple(VMEM for _ in outs),
        scratch_shapes=list(scratch),
        name=name,
        compiler_params=pltpu.CompilerParams(vmem_limit_bytes=room * 1024 * 1024),
    )

    def placed(*args):
        return run(
            *(
                pltpu.with_memory_space_constraint(x, pltpu.VMEM) if spec is HELD else x
                for x, spec in zip(args, ins)
            )
        )

    return placed


def side_strips(tiles):
    rows = tiles[0][0].shape[0]
    lane = iota((rows, LANES), 1)
    left = jnp.zeros((rows, LANES), jnp.float32)
    right = left
    for f, (first, last) in enumerate(tiles):
        mine = (lane >= f * HALO) & (lane < (f + 1) * HALO)
        left = jnp.where(mine, pltpu.roll(first, f * HALO, 1) if f else first, left)
        right = jnp.where(mine, pltpu.roll(last, f * HALO + HALO, 1), right)
    return left, right


def side_tile(from_east, from_west, f):
    lane = iota(from_east.shape, 1)
    east = pltpu.roll(from_east, (LANES - f * HALO) % LANES, 1) if f else from_east
    west = pltpu.roll(from_west, LANES - HALO - f * HALO, 1)
    return jnp.where(lane < HALO, east, jnp.where(lane >= LANES - HALO, west, 0.0))


def three_parts(x):
    high = x.astype(jnp.bfloat16)
    rest = x - high.astype(jnp.float32)
    middle = rest.astype(jnp.bfloat16)
    low = (rest - middle.astype(jnp.float32)).astype(jnp.bfloat16)
    return high, middle, low


def one_hot(pick):
    return jnp.where(pick, 1.0, 0.0).astype(jnp.bfloat16)


def dot(a, b):
    return jnp.dot(a, b, preferred_element_type=jnp.float32)


def exact_pick(pick, x):
    pick = one_hot(pick)
    high, middle, low = three_parts(x)
    return dot(pick, low) + dot(pick, middle) + dot(pick, high)


def all_fields(ca, vo, co):
    return [ca.at[0], ca.at[1], vo.at[0], vo.at[1], co]


def strips_kernel(ca, vo, co, to_west, to_east):
    left, right = side_strips([(f[:, :LANES], f[:, LANES:]) for f in all_fields(ca, vo, co)])
    to_west[...] = jnp.transpose(left)[: 5 * HALO]
    to_east[...] = jnp.transpose(right)[: 5 * HALO]


def sides_kernel(from_east, from_west, sides):
    blank = jnp.zeros((LANES - 5 * HALO, LANES), jnp.float32)
    east = jnp.transpose(jnp.concatenate([from_east[...], blank], axis=0))
    west = jnp.transpose(jnp.concatenate([from_west[...], blank], axis=0))
    for f in range(5):
        sides[f] = side_tile(east, west, f)


def lanes_to(x, source, target, count):
    lane = iota(x.shape, 1)
    turned = pltpu.roll(x, (target - source) % LANES, 1) if target != source else x
    return jnp.where((lane >= target) & (lane < target + count), turned, 0.0)


def pack_kernel(count, cells, partner, target, row, fluid, packed):
    i_circ = lax.axis_index("circ")
    i_axial = lax.axis_index("axial")
    slots = fluid.shape[0] // 4
    t_row = target[...]
    order = iota((1, slots), 1)
    used = order < count[0]
    eye = iota((slots, slots), 0) == iota((slots, slots), 1)
    both = jnp.sum(jnp.where(eye, t_row * 256 + row[...], 0), axis=1, keepdims=True)
    t_col = lax.shift_right_logical(both, 8)
    row_col = ((both & 255) + 1).astype(jnp.float32).astype(jnp.bfloat16)
    earlier = (
        (t_col == t_row)
        & (iota((slots, slots), 0) < count[0])
        & (iota((slots, slots), 0) < iota((slots, slots), 1))
    )
    rank = jnp.sum(jnp.where(earlier, 1, 0), axis=0, keepdims=True)
    place = jnp.where(used, rank * 128 + t_row, -1)
    pick = iota((256, slots), 0) == place
    tags = dot(one_hot(pick), jnp.broadcast_to(row_col, (slots, LANES)))
    tags0, tags1 = tags[:128], tags[128:]
    tiles = [fluid[pl.ds(c * 2 + k, slots, stride=4), :] for k in range(2) for c in range(2)]
    moved = exact_pick(pick, jnp.concatenate(tiles, axis=1))
    for half in range(2):
        for part in range(4):
            packed[pl.ds(half * 4 + part, 128, stride=BLOCK), :] = moved[
                half * 128 : half * 128 + 128, part * LANES : part * LANES + LANES
            ]
    lane = iota((128, LANES), 1)
    tail = jnp.where(lane == 0, tags0, jnp.where(lane == 1, tags1, 0.0))
    for slot in range(8):
        cell = cells[slot]
        for base, value in (
            (8, i_circ * 128 + cell // 256),
            (16, i_axial * 256 + cell % 256),
            (24, partner[slot]),
        ):
            tail = jnp.where(lane == base + slot, value.astype(jnp.float32), tail)
    east = jnp.where(lane == 2, tags0, jnp.where(lane == 3, tags1, 0.0))
    west = jnp.where(lane == 4, tags0, jnp.where(lane == 5, tags1, 0.0))
    for half in range(2):
        rows = moved[half * 128 : half * 128 + 128]
        for k in range(2):
            first = rows[:, 2 * k * LANES : (2 * k + 1) * LANES]
            last = rows[:, (2 * k + 1) * LANES : (2 * k + 2) * LANES]
            east = east + lanes_to(first, 0, 32 + half * 16 + k * HALO, HALO)
            west = west + lanes_to(last, LANES - HALO, 64 + half * 16 + k * HALO, HALO)
    tail = tail + pltpu.roll(east, 127, 0) + pltpu.roll(west, 1, 0)
    packed[pl.ds(8, 128, stride=BLOCK), :] = tail


def force_kernel(got, ca, vo, co, sides, force, ports, to_north, to_south):
    tail = got[pl.ds(8, 128, stride=BLOCK), :]
    tail_t = jnp.transpose(tail)
    ports[...] = tail_t[8:32]
    line = iota((128, 128), 0).astype(jnp.float32) + 1.0

    def pair(k):
        return jnp.concatenate([tail_t[k : k + 1] == line, tail_t[k + 1 : k + 2] == line], axis=1)

    blocks = [
        jnp.concatenate(
            [got[pl.ds(half * 4 + part, 128, stride=BLOCK), :] for half in range(2)], axis=0
        )
        for part in range(4)
    ]
    total = exact_pick(pair(0), jnp.concatenate(blocks, axis=1))
    both = jnp.concatenate([tail, pltpu.roll(tail, LANES - 16, 1)], axis=0)
    both = jnp.concatenate(three_parts(both), axis=1)
    east, west = dot(one_hot(pair(2)), both), dot(one_hot(pair(4)), both)
    east, west = [x[:, 256:] + x[:, 128:256] + x[:, :128] for x in (east, west)]
    coefs = []
    for tile in range(3):
        if tile < 2:
            shear = total[:, tile * LANES : (tile + 1) * LANES]
            agonist = total[:, (tile + 2) * LANES : (tile + 3) * LANES]
        else:
            shear, agonist = [
                lanes_to(east, 32 + k * HALO, 0, HALO)
                + lanes_to(west, 64 + k * HALO, LANES - HALO, HALO)
                for k in range(2)
            ]
        stress = shear * shear / (1.0 + shear * shear)
        stimulus = 0.5 + 0.5 * jnp.tanh(0.5 * agonist)
        a_s = 0.1 * stimulus
        a_e = 0.02 + 0.15 * stress + 0.04 * stimulus
        coefs.append((a_s, a_e))
        for f in range(2):
            force[f, tile] = coefs[tile][f]
    refs = all_fields(ca, vo, co)
    for rows, out in ((slice(0, HALO), to_north), (slice(128 - HALO, 128), to_south)):
        ends = jnp.zeros((HALO, LANES), jnp.float32)
        for f in range(7):
            for tile in range(2):
                out[2 * f + tile] = (
                    refs[f][rows, tile * LANES : (tile + 1) * LANES]
                    if f < 5
                    else coefs[tile][f - 5][rows]
                )
            side = sides[f, rows, :] if f < 5 else coefs[2][f - 5][rows]
            ends = ends + lanes_to(side, 0, f * 16, HALO)
            ends = ends + lanes_to(side, LANES - HALO, f * 16 + HALO, HALO)
        out[14] = ends


def strip_tiles(strip, f):
    ends = strip[14]
    side = lanes_to(ends, f * 16, 0, HALO) + lanes_to(ends, f * 16 + HALO, LANES - HALO, HALO)
    return [strip[2 * f], strip[2 * f + 1], side]


def extract(fields, cells, table, tmp, out):
    lane = iota((8, LANES), 1)
    long_lane = iota((16, LANES), 1)
    flat = fields.reshape(3 * 7 * EXT, LANES)
    for slot in range(8):
        cell = cells[slot]
        row = lax.shift_right_logical(cell, 8) + (HALO - RADIUS)
        col = (cell & 255) - RADIUS
        col = jnp.where(col < 0, col + WIDE, col)
        base = pl.multiple_of(row & -8, 8)
        turn = 16 - (row & 7)
        tile = lax.shift_right_logical(col, 7)
        other = jnp.where(tile == 2, 0, tile + 1)
        inside = col & (LANES - 1)
        kept = jnp.zeros((8, LANES), jnp.float32)
        span = 6 * EXT + 16
        here = flat.at[pl.ds(pl.multiple_of(tile * (7 * EXT) + base, 8), span), :]
        there = flat.at[pl.ds(pl.multiple_of(other * (7 * EXT) + base, 8), span), :]
        back = (LANES - inside) & (LANES - 1)
        for f, field in enumerate((2, 0, 3, 5, 1, 6, 4)):
            rows = slice(field * EXT, field * EXT + 16)
            window = jnp.where(long_lane < inside, there[rows, :], here[rows, :])
            window = pltpu.roll(pltpu.roll(window, turn, 0)[:8], back, 1)
            window = pltpu.roll(window, f * SIDE, 1) if f else window
            kept = jnp.where((lane >= f * SIDE) & (lane < (f + 1) * SIDE), window, kept)
        tmp[slot * 8 : slot * 8 + 8, :] = kept
    width = 2 * LANES
    at = iota((LANES, width), 0)
    wanted = table[0:1, :]
    pick = one_hot((at == wanted) | (at == wanted + 40) | (at == wanted + 80))
    high, middle, low = [x.astype(jnp.float32) for x in three_parts(tmp[...])]
    pieces = dot(
        (high + pltpu.roll(middle, 40, 1) + pltpu.roll(low, 80, 1)).astype(jnp.bfloat16), pick
    )
    mine = iota((64, width), 0) == table[1:2, :]
    line = jnp.sum(jnp.where(mine, pieces, 0.0), axis=0, keepdims=True)
    for k in range(2):
        out[pl.ds(k, 128, stride=2), :] = jnp.broadcast_to(
            line[:, k * LANES : (k + 1) * LANES], (128, LANES)
        )


class Field:
    def __init__(self, ref, f):
        self.ref, self.f = ref, f

    def __getitem__(self, at):
        return self.ref[(at[0], self.f) + at[1:]]

    def __setitem__(self, at, value):
        self.ref[(at[0], self.f) + at[1:]] = value


def fields_of(ref, count):
    return [Field(ref, f) for f in range(count)]


def build_rows(dst, tiles, north, south):
    for tile in range(3):
        dst[tile, slice(HALO, HALO + 128), :] = tiles[tile]
        dst[tile, slice(0, HALO), :] = north[tile]
        dst[tile, slice(HALO + 128, EXT), :] = south[tile]


def rows_at(j):
    return pl.ds(j, 8, stride=STEP)


def mixed_at(j):
    return pl.ds(8 * j, 8)


def to_mixed(src, dst):
    for tile in range(3):
        for j in range(STEP):
            dst[tile, mixed_at(j), :] = src[tile, rows_at(j), :]


def tables_kernel(ports, in_row, in_col, codes):
    rows, cols, _ = port_places(ports)
    make_codes(rows, cols, codes)
    i_circ = lax.axis_index("circ")
    i_axial = lax.axis_index("axial")
    row = my_column(rows.astype(jnp.float32)).astype(jnp.int32)
    col = my_column(cols.astype(jnp.float32)).astype(jnp.int32)
    row = (row - i_circ * 128 + HALO) & 1023
    col = col - i_axial * 256
    ok = (iota((NEAR_PORTS, 1), 0) < 72) & (col >= -HALO) & (col < 256 + HALO) & (row < EXT)
    col = jnp.where(ok, jnp.where(col < 0, col + WIDE, col), -1)
    group = lax.shift_right_logical(row * 57, 10)
    place = jnp.where(ok, (row - group * STEP) * 8 + group, -1)
    in_col[...] = jnp.where(col == iota((NEAR_PORTS, WIDE), 1), 1.0, 0.0)
    place = jnp.concatenate([place, place, place, jnp.full((16, 1), -1, jnp.int32)], axis=0)
    in_row[...] = jnp.transpose(jnp.where(place == iota((256, 256), 1), 1.0, 0.0))[:EXT]


def first_patch_kernel(
    cells, ca, vo, co, sides, from_north, from_south, force, table,
    ahead, coef, out, start, tmp,
):
    after = fields_of(ahead, 7)
    before = fields_of(start, 5)
    for f, ref in enumerate(all_fields(ca, vo, co)):
        scale = 0.05 if f == 4 else 1.0
        build_rows(
            before[f] if f < 4 else after[5],
            [t * scale for t in (ref[:, :LANES], ref[:, LANES:], sides[f])],
            [t * scale for t in strip_tiles(from_north, f)],
            [t * scale for t in strip_tiles(from_south, f)],
        )
    for f in range(2):
        build_rows(
            after[6] if f == 0 else before[4],
            [force[f, tile] for tile in range(3)],
            strip_tiles(from_north, 5 + f),
            strip_tiles(from_south, 5 + f),
        )
    for tile in range(3):
        ahead[tile, 4] = start[tile, 2]
    coefs = fields_of(coef, 3)
    for src, dst in zip((after[5], after[6], before[4]), coefs):
        to_mixed(src, dst)
    one_step(before[:4], rows_at, after[:4], rows_at, coefs, None)
    extract(ahead, cells, table, tmp, out)


def port_places(ports):
    return [ports[k * 8 : k * 8 + 8, :].astype(jnp.int32) for k in range(3)]


def port_sim(got, codes, rows, cols, partner):
    got_t = [jnp.transpose(got[pl.ds(k, 128, stride=2), :]) for k in range(2)]
    fields = [{} for _ in range(7)]
    for index, (field, cell) in enumerate(patch_plan()):
        at = index * 8 % LANES
        fields[field][cell] = got_t[index * 8 // LANES][at : at + 8]
    v, s, u, spread, e, a_s, before = fields
    device = partner // 8
    slot = partner % 8

    def near(f, cell):
        a, b = cell
        left = jnp.where(cols == -b, f[cell], f[(a, b - 1)])
        right = jnp.where(cols == 4095 - b, f[cell], f[(a, b + 1)])
        return f[(a - 1, b)] + f[(a + 1, b)] + left + right

    def gain_of(here):
        theirs = jnp.zeros_like(here)
        for k in range(8):
            line = jnp.broadcast_to(here[k : k + 1], here.shape)
            theirs = jnp.where(slot == k, jnp.take_along_axis(line, device, axis=1), theirs)
        return 0.2 * (theirs - here)

    def add_gain(f, gain, reach):
        added = dict(f)
        for k in range(8):
            turned = pltpu.roll(gain, k, 0) if k else gain
            for place, shift in enumerate(NEAR_LANES):
                cells = reachable(shift, reach)
                if not cells:
                    continue
                moved = pltpu.roll(turned, (-shift) % LANES, 1) if shift else turned
                code = codes[k * len(NEAR_LANES) + place]
                for c in cells:
                    key = (c[0] * ROW_KEY + c[1]) & KEY_MASK
                    added[c] = added[c] + jnp.where(code == key, moved, 0.0)
        return added

    gains = [gain_of(before[(0, 0)])]
    v = add_gain(v, gains[0], RADIUS)
    for step in range(RADIUS + 1):
        gains.append(gain_of(v[(0, 0)]))
        reach = RADIUS - 1 - step
        if reach < 0:
            break
        parts = {c: reciprocals(s[c], e.get(c)) for c in diamond(reach)}
        new_v = {}
        for c in diamond(reach):
            new_v[c] = v_step(parts[c], v[c], u[c], near(v, c), spread[c])
        new_s, new_u = {}, {}
        for c in diamond(reach - 1):
            new_s[c] = s_step(parts[c], s[c], e[c], v[c], near(s, c), spread[c], a_s[c])
            new_u[c] = u_step(parts[c], v[c], u[c], near(u, c), spread[c])
        v = add_gain(new_v, gains[-1], reach)
        s, u = new_s, new_u
    return gains


def reciprocals(s, e):
    half, whole = s + 0.5, s + 1.0
    both = half * whole
    if e is None:
        inv = 1.0 / both
        return inv * whole, inv * half, None
    end = e + 1.0
    inv = 1.0 / (both * end)
    rest = inv * end
    return rest * whole, rest * half, inv * both


def s_step(parts, s, e, v, near, spread, a_s):
    return (
        a_s
        + s * (0.97 - 4.0 * spread)
        + 0.03 * e
        - 0.08
        + 0.04 * jnp.tanh(v + 0.3)
        + 0.06 * parts[0]
        + spread * near
    )


def e_step(s, e, near, spread, a_e):
    return a_e + e * (0.88 - 4.0 * spread) + 0.03 * s + spread * near


def v_step(parts, v, u, near, spread):
    return (
        v * (0.71 - 4.0 * spread + 0.15 * parts[1])
        + 0.18 * parts[1]
        - 0.23
        + 0.04 * u
        + spread * near
    )


def u_step(parts, v, u, near, spread):
    return (
        u * (0.78 - 4.0 * spread + 0.1 * parts[2])
        + 0.12 * parts[2]
        - 0.152
        + 0.04 * v
        + spread * near
    )


def make_codes(rows, cols, codes):
    key = rows * ROW_KEY + cols
    index = 0
    for k in range(8):
        turned = pltpu.roll(key, k, 0) if k else key
        for shift in NEAR_LANES:
            moved = pltpu.roll(turned, (-shift) % LANES, 1) if shift else turned
            codes[index] = (moved - key) & KEY_MASK
            index += 1


def my_column(value):
    lane_of = lax.axis_index("circ") * 16 + lax.axis_index("axial")
    tiles = []
    lane = iota((8, LANES), 1)
    for shift in NEAR_LANES:
        at = (lane_of + shift) & (LANES - 1)
        tiles.append(jnp.sum(jnp.where(lane == at, value, 0.0), axis=1, keepdims=True))
    tiles.append(jnp.zeros((NEAR_PORTS - 8 * len(tiles), 1), jnp.float32))
    return jnp.concatenate(tiles, axis=0)


def injections(gains, in_row, in_col, inject):
    pick = in_row[...].astype(jnp.bfloat16)
    lane_of = lax.axis_index("circ") * 16 + lax.axis_index("axial")
    zero = jnp.zeros((NEAR_PORTS - 8 * len(NEAR_LANES), WIDE), jnp.float32)
    blank = jnp.zeros((256 - 3 * NEAR_PORTS, WIDE), jnp.bfloat16)
    for k, gain in enumerate(gains):
        lines = []
        for place, shift in enumerate(NEAR_LANES):
            at = jnp.zeros((8, LANES), jnp.int32) + ((lane_of + shift) & (LANES - 1))
            mine = jnp.take_along_axis(gain, at, axis=1)
            rows = slice(place * 8, place * 8 + 8)
            lines.append(in_col[rows, :] * jnp.concatenate([mine] * 3, axis=1))
        parts = three_parts(jnp.concatenate(lines + [zero], axis=0))
        total = dot(pick, jnp.concatenate(list(parts) + [blank], axis=0))
        for tile in range(3):
            inject[k, tile] = total[:, tile * LANES : (tile + 1) * LANES]


def one_step(now, now_at, later, later_at, coef, inject):
    lane = iota((8, LANES), 1)
    i_axial = lax.axis_index("axial")
    head = lane == 0
    tail = lane == LANES - 1
    is_first = (lane * 0 + i_axial) == 0
    is_last = (lane * 0 + i_axial) == 15

    def load(f, tile, j):
        if j < 0:
            return pltpu.roll(now[f][tile, now_at(STEP - 1), :], 1, 0)
        if j == STEP:
            return pltpu.roll(now[f][tile, now_at(0), :], 7, 0)
        return now[f][tile, now_at(j), :]

    for j in range(STEP):
        mid, near = [], []
        for f in range(4):
            x = [load(f, tile, j) for tile in range(3)]
            left = [pltpu.roll(y, 1, 1) for y in x]
            right = [pltpu.roll(y, LANES - 1, 1) for y in x]
            lefts = [
                jnp.where(head, jnp.where(is_first, x[0], left[2]), left[0]),
                jnp.where(head, left[0], left[1]),
                jnp.where(head, left[1], left[2]),
            ]
            rights = [
                jnp.where(tail, right[1], right[0]),
                jnp.where(tail, jnp.where(is_last, x[1], right[2]), right[1]),
                jnp.where(tail, right[0], right[2]),
            ]
            mid.append(x)
            near.append(
                [
                    (load(f, tile, j - 1) + load(f, tile, j + 1)) + (lefts[tile] + rights[tile])
                    for tile in range(3)
                ]
            )
        for tile in range(3):
            s, e, v, u = [x[tile] for x in mid]
            n = [x[tile] for x in near]
            spread = coef[0][tile, mixed_at(j), :]
            parts = reciprocals(s, e)
            new_s = s_step(parts, s, e, v, n[0], spread, coef[1][tile, mixed_at(j), :])
            new_e = e_step(s, e, n[1], spread, coef[2][tile, mixed_at(j), :])
            new_v = v_step(parts, v, u, n[2], spread)
            if inject is not None:
                new_v = new_v + inject[tile, mixed_at(j), :]
            later[0][tile, later_at(j), :] = new_s
            later[1][tile, later_at(j), :] = new_e
            later[2][tile, later_at(j), :] = new_v
            later[3][tile, later_at(j), :] = u_step(parts, v, u, n[3], spread)


def coupled_steps(ahead, coef, got, ports, in_row, in_col, codes, first, second, inject):
    rows, cols, partner = port_places(ports)
    gains = port_sim(got, codes, rows, cols, partner)
    injections(gains, in_row, in_col, inject)
    one, two = fields_of(first, 4), fields_of(second, 4)
    for f in range(4):
        for tile in range(3):
            for j in range(STEP):
                value = ahead[tile, f, rows_at(j), :]
                if f == 2:
                    value = value + inject[0, tile, mixed_at(j), :]
                first[tile, f, mixed_at(j), :] = value
    coefs = fields_of(coef, 3)
    for k, (now, later) in enumerate(((one, two), (two, one), (one, two))):
        one_step(now, mixed_at, later, mixed_at, coefs, inject.at[k + 1])
    return two


def first_steps_kernel(
    cells, ahead, coef, got, ports, in_row, in_col, codes, table,
    later, out, first, second, inject, tmp,
):
    now = coupled_steps(ahead, coef, got, ports, in_row, in_col, codes, first, second, inject)
    for tile in range(3):
        for j in range(STEP):
            later[tile, 4, rows_at(j), :] = second[tile, 2, mixed_at(j), :]
        later[tile, 5] = ahead[tile, 5]
        later[tile, 6] = ahead[tile, 6]
    one_step(now, mixed_at, fields_of(later, 4), rows_at, fields_of(coef, 3), None)
    extract(later, cells, table, tmp, out)


def last_steps_kernel(
    ahead, coef, got, ports, in_row, in_col, codes, ca_out, vo_out, first, second, inject
):
    coupled_steps(ahead, coef, got, ports, in_row, in_col, codes, first, second, inject)
    for f in range(4):
        out = (ca_out, vo_out)[f // 2].at[f % 2]
        for tile in range(2):
            for j in range(STEP):
                first[tile, f, rows_at(j), :] = second[tile, f, mixed_at(j), :]
            out[:, tile * LANES : (tile + 1) * LANES] = first[tile, f, HALO : HALO + 128, :]


def shifted(value, axis, step, periodic):
    count = lax.axis_size(axis)
    pairs = [(i, i + step) for i in range(count)]
    if periodic:
        pairs = [(i, j % count) for i, j in pairs]
    return lax.ppermute(value, axis, [(i, j) for i, j in pairs if 0 <= j < count])


def swap_axial(to_west, to_east):
    return shifted(to_west, "axial", -1, False), shifted(to_east, "axial", 1, False)


def swap_circ(to_north, to_south):
    return shifted(to_south, "circ", 1, True), shifted(to_north, "circ", -1, True)


def stack(count):
    return (3, count, EXT, LANES)


def to_all(value):
    blocks = value.reshape(128, 1, -1)
    return lax.all_to_all(blocks, AXES, 0, 0, tiled=True).reshape(value.shape)


def local(ca, vo, co, fluid, target, row, count, cells, partner):
    table = jnp.asarray(patch_table())
    lines = fluid.reshape(-1, 2, 2, LANES).transpose(0, 2, 1, 3).reshape(-1, LANES)
    (packed,) = call(pack_kernel, [(128 * BLOCK, LANES)], [SMEM] * 3 + [VMEM] * 3, "pack", room=60)(
        count, cells, partner, target.reshape(1, -1), row.reshape(1, -1), lines
    )
    received = to_all(packed)
    to_west, to_east = call(strips_kernel, [(5 * HALO, LANES)] * 2, [HELD] * 3, "strips")(
        ca, vo, co
    )
    from_east, from_west = swap_axial(to_west, to_east)
    (sides,) = call(sides_kernel, [(5, 128, LANES)], [HELD] * 2, "sides")(from_east, from_west)
    ring = (15, HALO, LANES)
    force, ports, to_north, to_south = call(
        force_kernel, [(2, 3, 128, LANES), (24, LANES), ring, ring], [HELD] * 5, "force"
    )(received, ca, vo, co, sides)
    from_north, from_south = swap_circ(to_north, to_south)
    in_row, in_col, codes = call(
        tables_kernel,
        [(EXT, 256), (NEAR_PORTS, WIDE), (72, 8, LANES)],
        [HELD],
        "tables",
        last=jnp.int32,
    )(ports)
    patch_space = pltpu.VMEM((64, LANES), jnp.float32)
    ahead, coef, patches = call(
        first_patch_kernel,
        [stack(7), stack(3), (256, LANES)],
        [SMEM] + [HELD] * 8,
        "first_patch",
        [pltpu.VMEM(stack(5), jnp.float32), patch_space],
    )(cells, ca, vo, co, sides, from_north, from_south, force, table)
    got = to_all(patches)
    scratch = [pltpu.VMEM(stack(4), jnp.float32)] * 2 + [pltpu.VMEM((4, 3, EXT, LANES), jnp.float32)]
    ahead, patches = call(
        first_steps_kernel,
        [stack(7), (256, LANES)],
        [SMEM] + [HELD] * 8,
        "first_steps",
        scratch + [patch_space],
    )(cells, ahead, coef, got, ports, in_row, in_col, codes, table)
    got = to_all(patches)
    return call(
        last_steps_kernel,
        [(2, 128, 256)] * 2,
        [HELD] * 7,
        "last_steps",
        scratch,
        place=jax.ShapeDtypeStruct,
    )(ahead, coef, got, ports, in_row, in_col, codes)


def solution(mesh):
    return jax.shard_map(
        local,
        mesh=mesh,
        in_specs=(
            P(None, "circ", "axial"),
            P(None, "circ", "axial"),
            P("circ", "axial"),
            P(AXES, None, None),
            P(AXES, None),
            P(AXES),
            P(AXES),
            P(AXES),
            P(AXES),
        ),
        out_specs=(P(None, "circ", "axial"), P(None, "circ", "axial")),
        check_vma=False,
    )
```

```python
import functools

import jax
import jax.numpy as jnp
import numpy as np
from jax import lax
from jax.experimental import pallas as pl
from jax.experimental.pallas import tpu as pltpu
from jax.sharding import PartitionSpec as P

AXES = ("circ", "axial")
HALO = 8
LANES = 128
WIDE = 384
RADIUS = 2
REACH = 3
SIDE = 5
BLOCK = 9
EXT = 144
STEP = 18
NEAR_PORTS = 80
NEAR_LANES = (0, 1, -1, 16, -16, 15, -15, 17, -17)
ROW_KEY = 8192
KEY_MASK = 1024 * ROW_KEY - 1
VMEM = pl.BlockSpec(memory_space=pltpu.VMEM)
SMEM = pl.BlockSpec(memory_space=pltpu.SMEM)


def diamond(radius):
    if radius < 0:
        return []
    span = range(-radius, radius + 1)
    return [(a, b) for a in span for b in span if abs(a) + abs(b) <= radius]


def reachable(shift, radius):
    down = {-17: -1, -16: -1, -15: -1, 15: 1, 16: 1, 17: 1}.get(shift, 0)
    right = {-17: -1, -1: -1, 15: -1, -15: 1, 1: 1, 17: 1}.get(shift, 0)
    return [(a, b) for a, b in diamond(radius) if a * down >= abs(down) and b * right >= abs(right)]


def patch_plan():
    radii = (2, 1, 1, 1, 0, 0, 0)
    return [(field, cell) for field, r in enumerate(radii) for cell in diamond(r)]


def patch_table():
    table = np.full((8, 2 * LANES), -1, np.int32)
    for index, (field, (a, b)) in enumerate(patch_plan()):
        for slot in range(8):
            at = index * 8 + slot
            table[0, at] = field * SIDE + b + RADIUS
            table[1, at] = slot * 8 + a + REACH
    return table


def iota(shape, dim):
    return lax.broadcasted_iota(jnp.int32, shape, dim)


HELD = pl.BlockSpec(memory_space=pltpu.VMEM)


def call(kernel, outs, ins, name, scratch=(), last=jnp.float32, place=pltpu.VMEM, room=20):
    types = [jnp.float32] * (len(outs) - 1) + [last]
    run = pl.pallas_call(
        kernel,
        out_shape=tuple(place(s, t) for s, t in zip(outs, types)),
        in_specs=ins,
        out_specs=tuple(VMEM for _ in outs),
        scratch_shapes=list(scratch),
        name=name,
        compiler_params=pltpu.CompilerParams(vmem_limit_bytes=room * 1024 * 1024),
    )

    def placed(*args):
        return run(
            *(
                pltpu.with_memory_space_constraint(x, pltpu.VMEM) if spec is HELD else x
                for x, spec in zip(args, ins)
            )
        )

    return placed


def side_strips(tiles):
    rows = tiles[0][0].shape[0]
    lane = iota((rows, LANES), 1)
    left = jnp.zeros((rows, LANES), jnp.float32)
    right = left
    for f, (first, last) in enumerate(tiles):
        mine = (lane >= f * HALO) & (lane < (f + 1) * HALO)
        left = jnp.where(mine, pltpu.roll(first, f * HALO, 1) if f else first, left)
        right = jnp.where(mine, pltpu.roll(last, f * HALO + HALO, 1), right)
    return left, right


def side_tile(from_east, from_west, f):
    lane = iota(from_east.shape, 1)
    east = pltpu.roll(from_east, (LANES - f * HALO) % LANES, 1) if f else from_east
    west = pltpu.roll(from_west, LANES - HALO - f * HALO, 1)
    return jnp.where(lane < HALO, east, jnp.where(lane >= LANES - HALO, west, 0.0))


def three_parts(x):
    high = x.astype(jnp.bfloat16)
    rest = x - high.astype(jnp.float32)
    middle = rest.astype(jnp.bfloat16)
    low = (rest - middle.astype(jnp.float32)).astype(jnp.bfloat16)
    return high, middle, low


def one_hot(pick):
    return jnp.where(pick, 1.0, 0.0).astype(jnp.bfloat16)


def dot(a, b):
    return jnp.dot(a, b, preferred_element_type=jnp.float32)


def exact_pick(pick, x):
    pick = one_hot(pick)
    high, middle, low = three_parts(x)
    return dot(pick, low) + dot(pick, middle) + dot(pick, high)


def all_fields(ca, vo, co):
    return [ca.at[0], ca.at[1], vo.at[0], vo.at[1], co]


def strips_kernel(ca, vo, co, to_west, to_east):
    left, right = side_strips([(f[:, :LANES], f[:, LANES:]) for f in all_fields(ca, vo, co)])
    to_west[...] = jnp.transpose(left)[: 5 * HALO]
    to_east[...] = jnp.transpose(right)[: 5 * HALO]


def sides_kernel(from_east, from_west, sides):
    blank = jnp.zeros((LANES - 5 * HALO, LANES), jnp.float32)
    east = jnp.transpose(jnp.concatenate([from_east[...], blank], axis=0))
    west = jnp.transpose(jnp.concatenate([from_west[...], blank], axis=0))
    for f in range(5):
        sides[f] = side_tile(east, west, f)


def lanes_to(x, source, target, count):
    lane = iota(x.shape, 1)
    turned = pltpu.roll(x, (target - source) % LANES, 1) if target != source else x
    return jnp.where((lane >= target) & (lane < target + count), turned, 0.0)


def pack_kernel(count, cells, partner, target, row, fluid, packed):
    i_circ = lax.axis_index("circ")
    i_axial = lax.axis_index("axial")
    slots = fluid.shape[0] // 4
    t_row = target[...]
    order = iota((1, slots), 1)
    used = order < count[0]
    eye = iota((slots, slots), 0) == iota((slots, slots), 1)
    both = jnp.sum(jnp.where(eye, t_row * 256 + row[...], 0), axis=1, keepdims=True)
    t_col = lax.shift_right_logical(both, 8)
    row_col = ((both & 255) + 1).astype(jnp.float32).astype(jnp.bfloat16)
    earlier = (
        (t_col == t_row)
        & (iota((slots, slots), 0) < count[0])
        & (iota((slots, slots), 0) < iota((slots, slots), 1))
    )
    rank = jnp.sum(jnp.where(earlier, 1, 0), axis=0, keepdims=True)
    place = jnp.where(used, rank * 128 + t_row, -1)
    pick = iota((256, slots), 0) == place
    tags = dot(one_hot(pick), jnp.broadcast_to(row_col, (slots, LANES)))
    tags0, tags1 = tags[:128], tags[128:]
    tiles = [fluid[pl.ds(c * 2 + k, slots, stride=4), :] for k in range(2) for c in range(2)]
    moved = exact_pick(pick, jnp.concatenate(tiles, axis=1))
    for half in range(2):
        for part in range(4):
            packed[pl.ds(half * 4 + part, 128, stride=BLOCK), :] = moved[
                half * 128 : half * 128 + 128, part * LANES : part * LANES + LANES
            ]
    lane = iota((128, LANES), 1)
    tail = jnp.where(lane == 0, tags0, jnp.where(lane == 1, tags1, 0.0))
    for slot in range(8):
        cell = cells[slot]
        for base, value in (
            (8, i_circ * 128 + cell // 256),
            (16, i_axial * 256 + cell % 256),
            (24, partner[slot]),
        ):
            tail = jnp.where(lane == base + slot, value.astype(jnp.float32), tail)
    east = jnp.where(lane == 2, tags0, jnp.where(lane == 3, tags1, 0.0))
    west = jnp.where(lane == 4, tags0, jnp.where(lane == 5, tags1, 0.0))
    for half in range(2):
        rows = moved[half * 128 : half * 128 + 128]
        for k in range(2):
            first = rows[:, 2 * k * LANES : (2 * k + 1) * LANES]
            last = rows[:, (2 * k + 1) * LANES : (2 * k + 2) * LANES]
            east = east + lanes_to(first, 0, 32 + half * 16 + k * HALO, HALO)
            west = west + lanes_to(last, LANES - HALO, 64 + half * 16 + k * HALO, HALO)
    tail = tail + pltpu.roll(east, 127, 0) + pltpu.roll(west, 1, 0)
    packed[pl.ds(8, 128, stride=BLOCK), :] = tail


def force_kernel(got, ca, vo, co, sides, force, ports, to_north, to_south):
    tail = got[pl.ds(8, 128, stride=BLOCK), :]
    tail_t = jnp.transpose(tail)
    ports[...] = tail_t[8:32]
    line = iota((128, 128), 0).astype(jnp.float32) + 1.0

    def pair(k):
        return jnp.concatenate([tail_t[k : k + 1] == line, tail_t[k + 1 : k + 2] == line], axis=1)

    blocks = [
        jnp.concatenate(
            [got[pl.ds(half * 4 + part, 128, stride=BLOCK), :] for half in range(2)], axis=0
        )
        for part in range(4)
    ]
    total = exact_pick(pair(0), jnp.concatenate(blocks, axis=1))
    both = jnp.concatenate([tail, pltpu.roll(tail, LANES - 16, 1)], axis=0)
    both = jnp.concatenate(three_parts(both), axis=1)
    east, west = dot(one_hot(pair(2)), both), dot(one_hot(pair(4)), both)
    east, west = [x[:, 256:] + x[:, 128:256] + x[:, :128] for x in (east, west)]
    coefs = []
    for tile in range(3):
        if tile < 2:
            shear = total[:, tile * LANES : (tile + 1) * LANES]
            agonist = total[:, (tile + 2) * LANES : (tile + 3) * LANES]
        else:
            shear, agonist = [
                lanes_to(east, 32 + k * HALO, 0, HALO)
                + lanes_to(west, 64 + k * HALO, LANES - HALO, HALO)
                for k in range(2)
            ]
        stress = shear * shear / (1.0 + shear * shear)
        stimulus = 0.5 + 0.5 * jnp.tanh(0.5 * agonist)
        a_s = 0.1 * stimulus
        a_e = 0.02 + 0.15 * stress + 0.04 * stimulus
        coefs.append((a_s, a_e))
        for f in range(2):
            force[f, tile] = coefs[tile][f]
    refs = all_fields(ca, vo, co)
    for rows, out in ((slice(0, HALO), to_north), (slice(128 - HALO, 128), to_south)):
        ends = jnp.zeros((HALO, LANES), jnp.float32)
        for f in range(7):
            for tile in range(2):
                out[2 * f + tile] = (
                    refs[f][rows, tile * LANES : (tile + 1) * LANES]
                    if f < 5
                    else coefs[tile][f - 5][rows]
                )
            side = sides[f, rows, :] if f < 5 else coefs[2][f - 5][rows]
            ends = ends + lanes_to(side, 0, f * 16, HALO)
            ends = ends + lanes_to(side, LANES - HALO, f * 16 + HALO, HALO)
        out[14] = ends


def strip_tiles(strip, f):
    ends = strip[14]
    side = lanes_to(ends, f * 16, 0, HALO) + lanes_to(ends, f * 16 + HALO, LANES - HALO, HALO)
    return [strip[2 * f], strip[2 * f + 1], side]


def extract(sources, cells, table, tmp, out):
    i_axial = lax.axis_index("axial")
    long_lane = iota((16, LANES), 1)
    lane = iota((64, LANES), 1)
    flats = {id(ref): ref.reshape(3 * n * EXT, LANES) for ref, n, _ in sources}
    marks = []
    for slot in range(8):
        cell = cells[slot]
        row = lax.shift_right_logical(cell, 8) + (HALO - REACH)
        own = cell & 255
        col = jnp.where(own < REACH, own + (WIDE - REACH), own - REACH)
        base = pl.multiple_of(row & -8, 8)
        turn = 16 - (row & 7)
        tile = lax.shift_right_logical(col, 7)
        other = jnp.where(tile == 2, 0, tile + 1)
        inside = col & (LANES - 1)
        back = (LANES - inside) & (LANES - 1)
        marks.append(jnp.zeros((8, LANES), jnp.int32) + own)
        views = {}
        for ref, n, _ in sources:
            if id(ref) not in views:
                span = (n - 1) * EXT + 16
                views[id(ref)] = [
                    flats[id(ref)].at[pl.ds(pl.multiple_of(t * (n * EXT) + base, 8), span), :]
                    for t in (tile, other)
                ]
        for f, (ref, _, field) in enumerate(sources):
            here, there = views[id(ref)]
            rows = slice(field * EXT, field * EXT + 16)
            window = jnp.where(long_lane < inside, there[rows, :], here[rows, :])
            tmp[f, slot * 8 : slot * 8 + 8, :] = pltpu.roll(
                pltpu.roll(window, turn, 0)[:8], back, 1
            )
    column = jnp.concatenate(marks, axis=0) + lane - REACH
    first = (column == 0) & ((lane * 0 + i_axial) == 0)
    last = (column == 255) & ((lane * 0 + i_axial) == 15)
    v, s, u, spread, e, a_s, a_e = [tmp[f] for f in range(7)]

    def near(x):
        left = jnp.where(first, x, pltpu.roll(x, 1, 1))
        right = jnp.where(last, x, pltpu.roll(x, LANES - 1, 1))
        return pltpu.roll(x, 1, 0) + pltpu.roll(x, 63, 0) + left + right

    parts = reciprocals(s, e)
    sent = [
        v_step(parts, v, u, near(v), spread),
        s_step(parts, s, e, v, near(s), spread, a_s),
        u_step(parts, v, u, near(u), spread),
        spread,
        e_step(s, e, near(e), spread, a_e),
        a_s,
        v,
    ]
    kept = jnp.zeros((64, LANES), jnp.float32)
    for f, value in enumerate(sent):
        moved = pltpu.roll(value, (f * SIDE + RADIUS - REACH) % LANES, 1)
        kept = jnp.where((lane >= f * SIDE) & (lane < (f + 1) * SIDE), moved, kept)
    width = 2 * LANES
    at = iota((LANES, width), 0)
    wanted = table[0:1, :]
    pick = one_hot((at == wanted) | (at == wanted + 40) | (at == wanted + 80))
    high, middle, low = [x.astype(jnp.float32) for x in three_parts(kept)]
    pieces = dot(
        (high + pltpu.roll(middle, 40, 1) + pltpu.roll(low, 80, 1)).astype(jnp.bfloat16), pick
    )
    mine = iota((64, width), 0) == table[1:2, :]
    line = jnp.sum(jnp.where(mine, pieces, 0.0), axis=0, keepdims=True)
    for k in range(2):
        out[pl.ds(k, 128, stride=2), :] = jnp.broadcast_to(
            line[:, k * LANES : (k + 1) * LANES], (128, LANES)
        )


class Field:
    def __init__(self, ref, f):
        self.ref, self.f = ref, f

    def __getitem__(self, at):
        return self.ref[(at[0], self.f) + at[1:]]

    def __setitem__(self, at, value):
        self.ref[(at[0], self.f) + at[1:]] = value


def fields_of(ref, count):
    return [Field(ref, f) for f in range(count)]


def build_rows(dst, tiles, north, south):
    for tile in range(3):
        dst[tile, slice(HALO, HALO + 128), :] = tiles[tile]
        dst[tile, slice(0, HALO), :] = north[tile]
        dst[tile, slice(HALO + 128, EXT), :] = south[tile]


def rows_at(j):
    return pl.ds(j, 8, stride=STEP)


def mixed_at(j):
    return pl.ds(8 * j, 8)


def to_mixed(src, dst):
    for tile in range(3):
        for j in range(STEP):
            dst[tile, mixed_at(j), :] = src[tile, rows_at(j), :]


def tables_kernel(ports, in_row, in_col, codes):
    rows, cols, _ = port_places(ports)
    make_codes(rows, cols, codes)
    i_circ = lax.axis_index("circ")
    i_axial = lax.axis_index("axial")
    row = my_column(rows.astype(jnp.float32)).astype(jnp.int32)
    col = my_column(cols.astype(jnp.float32)).astype(jnp.int32)
    row = (row - i_circ * 128 + HALO) & 1023
    col = col - i_axial * 256
    ok = (iota((NEAR_PORTS, 1), 0) < 72) & (col >= -HALO) & (col < 256 + HALO) & (row < EXT)
    col = jnp.where(ok, jnp.where(col < 0, col + WIDE, col), -1)
    group = lax.shift_right_logical(row * 57, 10)
    place = jnp.where(ok, (row - group * STEP) * 8 + group, -1)
    in_col[...] = jnp.where(col == iota((NEAR_PORTS, WIDE), 1), 1.0, 0.0)
    place = jnp.concatenate([place, place, place, jnp.full((16, 1), -1, jnp.int32)], axis=0)
    in_row[...] = jnp.transpose(jnp.where(place == iota((256, 256), 1), 1.0, 0.0))[:EXT]


ORDER = (2, 0, 3, 4, 1, 5, 6)


def first_patch_kernel(
    cells, ca, vo, co, sides, from_north, from_south, force, table, start, rest, out, tmp
):
    for f in range(7):
        scale = 0.05 if f == 4 else 1.0
        if f < 5:
            ref = all_fields(ca, vo, co)[f]
            tiles = [ref[:, :LANES], ref[:, LANES:], sides[f]]
        else:
            tiles = [force[f - 5, tile] for tile in range(3)]
        build_rows(
            Field(start, f) if f < 4 else Field(rest, f - 4),
            [t * scale for t in tiles],
            [t * scale for t in strip_tiles(from_north, f)],
            [t * scale for t in strip_tiles(from_south, f)],
        )
    extract(patch_sources(start, rest), cells, table, tmp, out)


def patch_sources(state, rest):
    return [(state, 4, f) if f < 4 else (rest, 3, f - 4) for f in ORDER]


def first_step_kernel(start, rest, ahead, coef):
    coefs = fields_of(coef, 3)
    for src, dst in zip(fields_of(rest, 3), coefs):
        to_mixed(src, dst)
    one_step(fields_of(start, 4), rows_at, fields_of(ahead, 4), mixed_at, coefs, None)


def free_step_kernel(state, coef, ahead):
    one_step(fields_of(state, 4), mixed_at, fields_of(ahead, 4), mixed_at, fields_of(coef, 3), None)


def port_places(ports):
    return [ports[k * 8 : k * 8 + 8, :].astype(jnp.int32) for k in range(3)]


def port_sim(got, codes, rows, cols, partner):
    got_t = [jnp.transpose(got[pl.ds(k, 128, stride=2), :]) for k in range(2)]
    fields = [{} for _ in range(7)]
    for index, (field, cell) in enumerate(patch_plan()):
        at = index * 8 % LANES
        fields[field][cell] = got_t[index * 8 // LANES][at : at + 8]
    v, s, u, spread, e, a_s, before = fields
    device = partner // 8
    slot = partner % 8

    def near(f, cell):
        a, b = cell
        left = jnp.where(cols == -b, f[cell], f[(a, b - 1)])
        right = jnp.where(cols == 4095 - b, f[cell], f[(a, b + 1)])
        return f[(a - 1, b)] + f[(a + 1, b)] + left + right

    def gain_of(here):
        theirs = jnp.zeros_like(here)
        for k in range(8):
            line = jnp.broadcast_to(here[k : k + 1], here.shape)
            theirs = jnp.where(slot == k, jnp.take_along_axis(line, device, axis=1), theirs)
        return 0.2 * (theirs - here)

    def add_gain(f, gain, reach):
        added = dict(f)
        for k in range(8):
            turned = pltpu.roll(gain, k, 0) if k else gain
            for place, shift in enumerate(NEAR_LANES):
                cells = reachable(shift, reach)
                if not cells:
                    continue
                moved = pltpu.roll(turned, (-shift) % LANES, 1) if shift else turned
                code = codes[k * len(NEAR_LANES) + place]
                for c in cells:
                    key = (c[0] * ROW_KEY + c[1]) & KEY_MASK
                    added[c] = added[c] + jnp.where(code == key, moved, 0.0)
        return added

    gains = [gain_of(before[(0, 0)])]
    v = add_gain(v, gains[0], RADIUS)
    for step in range(RADIUS + 1):
        gains.append(gain_of(v[(0, 0)]))
        reach = RADIUS - 1 - step
        if reach < 0:
            break
        parts = {c: reciprocals(s[c], e.get(c)) for c in diamond(reach)}
        new_v = {}
        for c in diamond(reach):
            new_v[c] = v_step(parts[c], v[c], u[c], near(v, c), spread[c])
        new_s, new_u = {}, {}
        for c in diamond(reach - 1):
            new_s[c] = s_step(parts[c], s[c], e[c], v[c], near(s, c), spread[c], a_s[c])
            new_u[c] = u_step(parts[c], v[c], u[c], near(u, c), spread[c])
        v = add_gain(new_v, gains[-1], reach)
        s, u = new_s, new_u
    return gains


def reciprocals(s, e):
    half, whole = s + 0.5, s + 1.0
    both = half * whole
    if e is None:
        inv = 1.0 / both
        return inv * whole, inv * half, None
    end = e + 1.0
    inv = 1.0 / (both * end)
    rest = inv * end
    return rest * whole, rest * half, inv * both


def s_step(parts, s, e, v, near, spread, a_s):
    return (
        a_s
        + s * (0.97 - 4.0 * spread)
        + 0.03 * e
        - 0.08
        + 0.04 * jnp.tanh(v + 0.3)
        + 0.06 * parts[0]
        + spread * near
    )


def e_step(s, e, near, spread, a_e):
    return a_e + e * (0.88 - 4.0 * spread) + 0.03 * s + spread * near


def v_step(parts, v, u, near, spread):
    return (
        v * (0.71 - 4.0 * spread + 0.15 * parts[1])
        + 0.18 * parts[1]
        - 0.23
        + 0.04 * u
        + spread * near
    )


def u_step(parts, v, u, near, spread):
    return (
        u * (0.78 - 4.0 * spread + 0.1 * parts[2])
        + 0.12 * parts[2]
        - 0.152
        + 0.04 * v
        + spread * near
    )


def make_codes(rows, cols, codes):
    key = rows * ROW_KEY + cols
    index = 0
    for k in range(8):
        turned = pltpu.roll(key, k, 0) if k else key
        for shift in NEAR_LANES:
            moved = pltpu.roll(turned, (-shift) % LANES, 1) if shift else turned
            codes[index] = (moved - key) & KEY_MASK
            index += 1


def my_column(value):
    lane_of = lax.axis_index("circ") * 16 + lax.axis_index("axial")
    tiles = []
    lane = iota((8, LANES), 1)
    for shift in NEAR_LANES:
        at = (lane_of + shift) & (LANES - 1)
        tiles.append(jnp.sum(jnp.where(lane == at, value, 0.0), axis=1, keepdims=True))
    tiles.append(jnp.zeros((NEAR_PORTS - 8 * len(tiles), 1), jnp.float32))
    return jnp.concatenate(tiles, axis=0)


def injections(gains, in_row, in_col, inject):
    pick = in_row[...].astype(jnp.bfloat16)
    lane_of = lax.axis_index("circ") * 16 + lax.axis_index("axial")
    zero = jnp.zeros((NEAR_PORTS - 8 * len(NEAR_LANES), WIDE), jnp.float32)
    blank = jnp.zeros((256 - 3 * NEAR_PORTS, WIDE), jnp.bfloat16)
    for k, gain in enumerate(gains):
        lines = []
        for place, shift in enumerate(NEAR_LANES):
            at = jnp.zeros((8, LANES), jnp.int32) + ((lane_of + shift) & (LANES - 1))
            mine = jnp.take_along_axis(gain, at, axis=1)
            rows = slice(place * 8, place * 8 + 8)
            lines.append(in_col[rows, :] * jnp.concatenate([mine] * 3, axis=1))
        parts = three_parts(jnp.concatenate(lines + [zero], axis=0))
        total = dot(pick, jnp.concatenate(list(parts) + [blank], axis=0))
        for tile in range(3):
            inject[k, tile] = total[:, tile * LANES : (tile + 1) * LANES]


def one_step(now, now_at, later, later_at, coef, inject):
    lane = iota((8, LANES), 1)
    i_axial = lax.axis_index("axial")
    head = lane == 0
    tail = lane == LANES - 1
    is_first = (lane * 0 + i_axial) == 0
    is_last = (lane * 0 + i_axial) == 15

    def load(f, tile, j):
        if j < 0:
            return pltpu.roll(now[f][tile, now_at(STEP - 1), :], 1, 0)
        if j == STEP:
            return pltpu.roll(now[f][tile, now_at(0), :], 7, 0)
        return now[f][tile, now_at(j), :]

    for j in range(STEP):
        mid, near = [], []
        for f in range(4):
            x = [load(f, tile, j) for tile in range(3)]
            left = [pltpu.roll(y, 1, 1) for y in x]
            right = [pltpu.roll(y, LANES - 1, 1) for y in x]
            lefts = [
                jnp.where(head, jnp.where(is_first, x[0], left[2]), left[0]),
                jnp.where(head, left[0], left[1]),
                jnp.where(head, left[1], left[2]),
            ]
            rights = [
                jnp.where(tail, right[1], right[0]),
                jnp.where(tail, jnp.where(is_last, x[1], right[2]), right[1]),
                jnp.where(tail, right[0], right[2]),
            ]
            mid.append(x)
            near.append(
                [
                    (load(f, tile, j - 1) + load(f, tile, j + 1)) + (lefts[tile] + rights[tile])
                    for tile in range(3)
                ]
            )
        for tile in range(3):
            s, e, v, u = [x[tile] for x in mid]
            n = [x[tile] for x in near]
            spread = coef[0][tile, mixed_at(j), :]
            parts = reciprocals(s, e)
            new_s = s_step(parts, s, e, v, n[0], spread, coef[1][tile, mixed_at(j), :])
            new_e = e_step(s, e, n[1], spread, coef[2][tile, mixed_at(j), :])
            new_v = v_step(parts, v, u, n[2], spread)
            if inject is not None:
                new_v = new_v + inject[tile, mixed_at(j), :]
            later[0][tile, later_at(j), :] = new_s
            later[1][tile, later_at(j), :] = new_e
            later[2][tile, later_at(j), :] = new_v
            later[3][tile, later_at(j), :] = u_step(parts, v, u, n[3], spread)


def coupled_steps(ahead, coef, got, ports, in_row, in_col, codes, first, second, inject):
    rows, cols, partner = port_places(ports)
    gains = port_sim(got, codes, rows, cols, partner)
    injections(gains, in_row, in_col, inject)
    one, two = fields_of(first, 4), fields_of(second, 4)
    now = fields_of(ahead, 4)
    for tile in range(3):
        first[tile, 2] = ahead[tile, 2] + inject[0, tile]
    now[2] = one[2]
    coefs = fields_of(coef, 3)
    one_step(now, mixed_at, two, mixed_at, coefs, inject.at[1])
    one_step(two, mixed_at, one, mixed_at, coefs, inject.at[2])
    one_step(one, mixed_at, two, mixed_at, coefs, inject.at[3])


def first_steps_kernel(
    cells, ahead, coef, rest, got, ports, in_row, in_col, codes, table,
    second, out, first, inject, tmp,
):
    coupled_steps(ahead, coef, got, ports, in_row, in_col, codes, first, second, inject)
    for f in range(4):
        for tile in range(3):
            for j in range(STEP):
                first[tile, f, rows_at(j), :] = second[tile, f, mixed_at(j), :]
    extract(patch_sources(first, rest), cells, table, tmp, out)


def last_steps_kernel(
    ahead, coef, got, ports, in_row, in_col, codes, ca_out, vo_out, first, second, inject
):
    coupled_steps(ahead, coef, got, ports, in_row, in_col, codes, first, second, inject)
    for f in range(4):
        out = (ca_out, vo_out)[f // 2].at[f % 2]
        for tile in range(2):
            for j in range(STEP):
                first[tile, f, rows_at(j), :] = second[tile, f, mixed_at(j), :]
            out[:, tile * LANES : (tile + 1) * LANES] = first[tile, f, HALO : HALO + 128, :]


def shifted(value, axis, step, periodic):
    count = lax.axis_size(axis)
    pairs = [(i, i + step) for i in range(count)]
    if periodic:
        pairs = [(i, j % count) for i, j in pairs]
    return lax.ppermute(value, axis, [(i, j) for i, j in pairs if 0 <= j < count])


def swap_axial(to_west, to_east):
    return shifted(to_west, "axial", -1, False), shifted(to_east, "axial", 1, False)


def swap_circ(to_north, to_south):
    return shifted(to_south, "circ", 1, True), shifted(to_north, "circ", -1, True)


def stack(count):
    return (3, count, EXT, LANES)


def to_all(value):
    blocks = value.reshape(128, 1, -1)
    return lax.all_to_all(blocks, AXES, 0, 0, tiled=True).reshape(value.shape)


def local(ca, vo, co, fluid, target, row, count, cells, partner):
    table = jnp.asarray(patch_table())
    lines = fluid.reshape(-1, 2, 2, LANES).transpose(0, 2, 1, 3).reshape(-1, LANES)
    (packed,) = call(pack_kernel, [(128 * BLOCK, LANES)], [SMEM] * 3 + [VMEM] * 3, "pack", room=60)(
        count, cells, partner, target.reshape(1, -1), row.reshape(1, -1), lines
    )
    received = to_all(packed)
    to_west, to_east = call(strips_kernel, [(5 * HALO, LANES)] * 2, [HELD] * 3, "strips")(
        ca, vo, co
    )
    from_east, from_west = swap_axial(to_west, to_east)
    (sides,) = call(sides_kernel, [(5, 128, LANES)], [HELD] * 2, "sides")(from_east, from_west)
    ring = (15, HALO, LANES)
    force, ports, to_north, to_south = call(
        force_kernel, [(2, 3, 128, LANES), (24, LANES), ring, ring], [HELD] * 5, "force"
    )(received, ca, vo, co, sides)
    from_north, from_south = swap_circ(to_north, to_south)
    in_row, in_col, codes = call(
        tables_kernel,
        [(EXT, 256), (NEAR_PORTS, WIDE), (72, 8, LANES)],
        [HELD],
        "tables",
        last=jnp.int32,
    )(ports)
    patch_space = pltpu.VMEM((7, 64, LANES), jnp.float32)
    start, rest, patches = call(
        first_patch_kernel,
        [stack(4), stack(3), (256, LANES)],
        [SMEM] + [HELD] * 8,
        "first_patch",
        [patch_space],
    )(cells, ca, vo, co, sides, from_north, from_south, force, table)
    got = to_all(patches)
    ahead, coef = call(first_step_kernel, [stack(4), stack(3)], [HELD] * 2, "first_step")(
        start, rest
    )
    moved = pltpu.VMEM(stack(4), jnp.float32)
    inject = pltpu.VMEM((4, 3, EXT, LANES), jnp.float32)
    state, patches = call(
        first_steps_kernel,
        [stack(4), (256, LANES)],
        [SMEM] + [HELD] * 7 + [VMEM] * 2,
        "first_steps",
        [moved, inject, patch_space],
    )(cells, ahead, coef, rest, got, ports, in_row, in_col, codes, table)
    got = to_all(patches)
    (ahead,) = call(free_step_kernel, [stack(4)], [HELD] * 2, "free_step")(state, coef)
    return call(
        last_steps_kernel,
        [(2, 128, 256)] * 2,
        [HELD] * 7,
        "last_steps",
        [moved, moved, inject],
        place=jax.ShapeDtypeStruct,
    )(ahead, coef, got, ports, in_row, in_col, codes)


def solution(mesh):
    return jax.shard_map(
        local,
        mesh=mesh,
        in_specs=(
            P(None, "circ", "axial"),
            P(None, "circ", "axial"),
            P("circ", "axial"),
            P(AXES, None, None),
            P(AXES, None),
            P(AXES),
            P(AXES),
            P(AXES),
            P(AXES),
        ),
        out_specs=(P(None, "circ", "axial"), P(None, "circ", "axial")),
        check_vma=False,
    )
```
